32 devices in a mesh: twin: 2 (over core), dp: 4 (over y, x), fsdp: 4 (over z).
Axes of the slice: x: 2, y: 2, z: 4, core: 2. Of those that a mesh axis runs over, the one named last changes fastest.
Arguments:
- tokens: bfloat16 [64, 512, 768], P(('twin', 'dp', 'fsdp')), may hold values from -6 to 6
- w_query: bfloat16 [768, 768], P('fsdp'), may hold values from -0.21875 to 0.21875
- b_query: bfloat16 [768], P('fsdp'), may hold values from -3 to 3
- w_key: bfloat16 [768, 768], P('fsdp'), may hold values from -0.21875 to 0.21875
- w_value: bfloat16 [768, 768], P('fsdp'), may hold values from -0.21875 to 0.21875
- b_value: bfloat16 [768], P('fsdp'), may hold values from -3 to 3
- w_out: bfloat16 [768, 768], P('fsdp'), may hold values from -0.875 to 0.875
- b_out: bfloat16 [768], P('fsdp'), may hold values from -3 to 3
- gain_attn: bfloat16 [768], P('fsdp'), may hold values from 0.5 to 1.5
- shift_attn: bfloat16 [768], P('fsdp'), may hold values from -2 to 2
- w_inner: bfloat16 [768, 3072], P('fsdp'), may hold values from -0.21875 to 0.21875
- b_inner: bfloat16 [3072], P('fsdp'), may hold values from -3 to 3
- w_outer: bfloat16 [3072, 768], P('fsdp'), may hold values from -0.109375 to 0.109375
- b_outer: bfloat16 [768], P('fsdp'), may hold values from -3 to 3
- gain_ffn: bfloat16 [768], P('fsdp'), may hold values from 0.5 to 1.5
- shift_ffn: bfloat16 [768], P('fsdp'), may hold values from -0.59765625 to 0.59765625
- lengths: int32 [64, 9], P(('twin', 'dp', 'fsdp')), may hold values from 1 to 128, 512 in all within a row
- labels: int32 [256], replicated, may hold values from 0 to 255, each once
Outputs:
- output: bfloat16 [64, 512, 768], P(('twin', 'dp', 'fsdp'))
- grad_tokens: bfloat16 [64, 512, 768], P(('twin', 'dp', 'fsdp'))
- grad_w_query: float32 [768, 768], P('fsdp')
- grad_b_query: float32 [768], P('fsdp')
- grad_w_key: float32 [768, 768], P('fsdp')
- grad_w_value: float32 [768, 768], P('fsdp')
- grad_b_value: float32 [768], P('fsdp')
- grad_w_out: float32 [768, 768], P('fsdp')
- grad_b_out: float32 [768], P('fsdp')
- grad_gain_attn: float32 [768], P('fsdp')
- grad_shift_attn: float32 [768], P('fsdp')
- grad_w_inner: float32 [768, 3072], P('fsdp')
- grad_b_inner: float32 [3072], P('fsdp')
- grad_w_outer: float32 [3072, 768], P('fsdp')
- grad_b_outer: float32 [768], P('fsdp')
- grad_gain_ffn: float32 [768], P('fsdp')
- grad_shift_ffn: float32 [768], P('fsdp')
The draws below stay inside these ranges and needn't reach their ends.
Inputs may be any that keep to these rules, and one draw needn't show every extreme that they name: `lengths`: each row's first 8 entries are the token counts of its sentences in order and the last is the count of its padding tokens; the entries of a row sum to 512. labels[i] is the positive sentence paired with anchor i; every positive is named by exactly one anchor.
All inputs are finite; a program needn't handle non-finite values.
Results may differ from the reference program's by a relative error of at most 0.02.
Values may be sent and summed in bfloat16 or wider, within the bound.
No kernel may reach another device: no remote copies, remote signals or barrier semaphores. Data moves between devices by JAX's collectives and lax.ppermute only.
A program may use at most 192 MiB of HBM per device.

```python
import math
import jax
import jax.numpy as jnp
import numpy as np
from jax import lax

D = 768
H = 12
HD = 64
FF = 3072
SEQ = 512
SEG = 8
MOST = 128
ROWS = 64
NA = 256


def shard_levels(key, dims, pieces, smallest, top_value):
    factor_of = 1.0
    for dim, shards_of in pieces:
        draws = jax.random.uniform(jax.random.fold_in(jax.random.fold_in(key, 6), dim), (shards_of,), jnp.float32, smallest / len(pieces), top_value / len(pieces))
        factor_of = factor_of * jnp.repeat(jnp.exp(draws), dims[dim] // shards_of).reshape((-1,) + (1,) * (len(dims) - 1 - dim))
    return factor_of


def split_up(count, total, limit, slope):
    weights = [(1 << 20) // math.isqrt(grade ** slope) + 1 for grade in range(2, count + 1)]
    spare, counts = total - limit - (count - 1), [1] * (count - 1)
    while spare > 0:
        candidates = [i for i in range(count - 1) if counts[i] < limit]
        pool, remaining = sum([weights[i] for i in candidates]), spare
        for i in candidates:
            extra = min(limit - counts[i], max(1, remaining * weights[i] // pool), spare)
            counts[i] = counts[i] + extra
            spare = spare - extra
    return np.array([limit] + counts)


def ragged(key, amount, total, bound, slope):
    if amount == 2:
        one = jax.random.randint(key, (), max(1, total - bound), min(bound, total - 1) + 1)
        return jnp.stack([one, total - one])
    sizes = jnp.asarray(split_up(amount, total, bound, slope), jnp.int32)
    pairs = (amount - 1) // 2
    source_of, sink = sizes[1:1 + 2 * pairs:2], sizes[2:2 + 2 * pairs:2]
    room = jnp.minimum(source_of - 1, bound - sink)
    passed = jax.random.randint(jax.random.fold_in(key, 1), (pairs,), 0, 1 << 20) % (room + 1)
    sizes = sizes.at[1:1 + 2 * pairs:2].set(source_of - passed).at[2:2 + 2 * pairs:2].set(sink + passed)
    return sizes[jax.random.permutation(jax.random.fold_in(key, 2), amount)]


def noise(rng, extent, scale, bound, cuts=(), kind=jnp.bfloat16):
    entries = scale * jax.random.normal(rng, extent, jnp.float32)
    if cuts:
        entries = entries * shard_levels(rng, extent, cuts, -0.22, 0.18)
    return jnp.clip(entries, -bound, bound).astype(kind)


def setup_inputs(seed: int = 0) -> dict:
    key_of = jax.random.split(jax.random.key(seed), 19)
    tokens = noise(key_of[0], (ROWS, SEQ, D), 1.0, 6.0, ((0, 32),))
    w_query = noise(key_of[1], (D, D), D ** -0.5, 0.21875, ((0, 4),))
    b_query = noise(key_of[2], (D,), 0.5, 3.0, ((0, 4),))
    w_key = noise(key_of[3], (D, D), D ** -0.5, 0.21875, ((0, 4),))
    w_value = noise(key_of[4], (D, D), D ** -0.5, 0.21875, ((0, 4),))
    b_value = noise(key_of[5], (D,), 0.5, 3.0, ((0, 4),))
    w_out = noise(key_of[6], (D, D), (D // 16) ** -0.5, 0.875, ((0, 4),))
    b_out = noise(key_of[7], (D,), 0.5, 3.0, ((0, 4),))
    gain_attn = jnp.clip(1.0 + 0.1 * jax.random.normal(key_of[8], (D,), jnp.float32), 0.5, 1.5).astype(jnp.bfloat16)
    shift_attn = noise(key_of[9], (D,), 0.3, 2.0, ((0, 4),))
    w_inner = noise(key_of[10], (D, FF), D ** -0.5, 0.21875, ((0, 4),))
    b_inner = noise(key_of[11], (FF,), 0.5, 3.0, ((0, 4),))
    w_outer = noise(key_of[12], (FF, D), FF ** -0.5, 0.109375, ((0, 4),))
    b_outer = noise(key_of[13], (D,), 0.5, 3.0, ((0, 4),))
    gain_ffn = jnp.clip(1.0 + 0.1 * jax.random.normal(key_of[14], (D,), jnp.float32), 0.5, 1.5).astype(jnp.bfloat16)
    shift_ffn = noise(key_of[15], (D,), 0.1, 0.59765625, ((0, 4),))
    lengths = jax.vmap(lambda own: ragged(own, SEG + 1, SEQ, MOST, 2))(jax.random.split(key_of[16], ROWS)).reshape((ROWS, SEG + 1)).astype(jnp.int32)
    labels = jax.random.permutation(key_of[17], NA).astype(jnp.int32)
    return {"tokens": tokens, "w_query": w_query, "b_query": b_query, "w_key": w_key, "w_value": w_value, "b_value": b_value, "w_out": w_out, "b_out": b_out, "gain_attn": gain_attn, "shift_attn": shift_attn, "w_inner": w_inner, "b_inner": b_inner, "w_outer": w_outer, "b_outer": b_outer, "gain_ffn": gain_ffn, "shift_ffn": shift_ffn, "lengths": lengths, "labels": labels}


norm_eps = 1e-12
pool_eps = 1e-06
sim_scale = 20.0
group_rows = 8

@jax.custom_vjp
def low(v):
    return lax.optimization_barrier(v.astype(jnp.bfloat16)).astype(jnp.float32)

@jax.custom_vjp
def low_back(v):
    return v

def low_keep(v):
    return (low(v), None)

def low_pass(kept, grad):
    return (grad,)

def back_keep(v):
    return (v, None)

def back_low(kept, grad):
    return (low(grad),)
low.defvjp(low_keep, low_pass)
low_back.defvjp(back_keep, back_low)

def exact_dot(left, right):
    return jnp.dot(left, right, precision=lax.Precision.HIGHEST)

def segment_ids(lengths):
    ends = jnp.cumsum(lengths, axis=1, dtype=jnp.int32)
    position = jnp.arange(SEQ, dtype=jnp.int32)
    return lax.optimization_barrier(jnp.sum((position[None, :, None] >= ends[:, None, :]).astype(jnp.int32), axis=2)).astype(jnp.int32)

def layer_norm(hidden, gain, shift):
    centred = hidden - lax.optimization_barrier(jnp.mean(hidden, axis=-1, keepdims=True))
    variance = lax.optimization_barrier(jnp.mean(centred * centred, axis=-1, keepdims=True))
    return centred * lax.rsqrt(variance + norm_eps) * gain + shift

def row_forward(row_tok, row_ids, params):
    w_query, b_query, w_key, w_value, b_value, w_out, b_out, gain_attn, shift_attn, w_inner, b_inner, w_outer, b_outer, gain_ffn, shift_ffn = params
    query = low(low_back(exact_dot(row_tok, w_query) + b_query)).reshape(SEQ, H, HD)
    keys = low(low_back(exact_dot(row_tok, w_key))).reshape(SEQ, H, HD)
    values = low(low_back(exact_dot(row_tok, w_value) + b_value)).reshape(SEQ, H, HD)
    scores = jnp.einsum('qhd,khd->hqk', query, keys, precision=lax.Precision.HIGHEST) * HD ** (-0.5)
    scores = low_back(scores)
    same = row_ids[:, None] == row_ids[None, :]
    scores = jnp.where(same[None], scores, -1e+30)
    attn_prob = jax.nn.softmax(scores, axis=-1)
    context = jnp.einsum('hqk,khd->qhd', low(attn_prob), values, precision=lax.Precision.HIGHEST)
    context = low(low_back(context.reshape(SEQ, D)))
    hidden = row_tok + exact_dot(context, w_out) + b_out
    mid_state = layer_norm(hidden, gain_attn, shift_attn)
    inner = low_back(exact_dot(low(mid_state), w_inner) + b_inner)
    activ = low(jax.nn.gelu(inner, approximate=False))
    branch = low_back(exact_dot(activ, w_outer) + b_outer)
    final = layer_norm(mid_state + branch, gain_ffn, shift_ffn)
    member = (row_ids[None, :] == jnp.arange(SEG, dtype=jnp.int32)[:, None]).astype(jnp.float32)
    pooled = exact_dot(member, final) / lax.optimization_barrier(jnp.sum(member, axis=1, keepdims=True))
    return (final, pooled)

def forward(tok_f, seg_ids, params):
    groups = tok_f.shape[0] // group_rows

    def one_group(item):
        group_tok, group_ids = item
        return jax.vmap(lambda row_tok, row_ids: row_forward(row_tok, row_ids, params))(group_tok, group_ids)
    final, pooled = lax.map(jax.checkpoint(one_group), (tok_f.reshape(groups, group_rows, SEQ, D), seg_ids.reshape(groups, group_rows, SEQ)))
    return (final.reshape(ROWS, SEQ, D), pooled.reshape(ROWS * SEG, D))

def contrast(pooled, labels):
    sent = low(pooled)
    unit = sent * lax.rsqrt(lax.optimization_barrier(jnp.sum(sent * sent, axis=1, keepdims=True)) + pool_eps)
    similar = sim_scale * exact_dot(unit[:NA], unit[NA:].T)
    match = labels[:, None] == jnp.arange(NA, dtype=jnp.int32)[None, :]
    row_part = jnp.sum(jax.nn.logsumexp(similar, axis=1))
    col_part = jnp.sum(jax.nn.logsumexp(similar, axis=0))
    return row_part + col_part - 2.0 * jnp.sum(jnp.where(match, similar, 0.0))

def reference(tokens, w_query, b_query, w_key, w_value, b_value, w_out, b_out, gain_attn, shift_attn, w_inner, b_inner, w_outer, b_outer, gain_ffn, shift_ffn, lengths, labels):
    seg_ids = segment_ids(lengths)
    params = tuple((weight.astype(jnp.float32) for weight in (w_query, b_query, w_key, w_value, b_value, w_out, b_out, gain_attn, shift_attn, w_inner, b_inner, w_outer, b_outer, gain_ffn, shift_ffn)))

    def objective(tok_f, weights):
        final, pooled = forward(tok_f, seg_ids, weights)
        return (contrast(pooled, labels), final)
    total, pull_back, final = jax.vjp(objective, tokens.astype(jnp.float32), params, has_aux=True)
    grad_tok, grads = pull_back(jnp.ones_like(total))
    return (final.astype(jnp.bfloat16), grad_tok.astype(jnp.bfloat16), grads[0], grads[1], grads[2], grads[3], grads[4], grads[5], grads[6], grads[7], grads[8], grads[9], grads[10], grads[11], grads[12], grads[13], grads[14])
```

```python
import functools

import jax
import jax.numpy as jnp
from jax import lax
from jax.sharding import PartitionSpec as P

H = 12
HD = 64
SEG = 8


norm_eps = 1e-12
pool_eps = 1e-06
sim_scale = 20.0


def cross_dot(left, right):
    return lax.dot_general(
        left, right, (((0,), (0,)), ((), ())), preferred_element_type=jnp.float32
    )


def back_dot(left, right):
    return lax.dot_general(
        left, right, (((1,), (1,)), ((), ())), preferred_element_type=jnp.float32
    )


def plain_dot(left, right):
    return jnp.dot(left, right, preferred_element_type=jnp.float32)


def segment_ids(lengths, seq_len):
    ends = jnp.cumsum(lengths, axis=1, dtype=jnp.int32)
    position = jnp.arange(seq_len, dtype=jnp.int32)
    return jnp.sum((position[None, :, None] >= ends[:, None, :]).astype(jnp.int32), axis=2)


def normalize(hidden):
    centred = hidden - jnp.mean(hidden, axis=-1, keepdims=True)
    inv_dev = lax.rsqrt(jnp.mean(centred * centred, axis=-1, keepdims=True) + norm_eps)
    return (centred * inv_dev, inv_dev)


def norm_back(grad_normed, normed, inv_dev):
    return inv_dev * (
        grad_normed
        - jnp.mean(grad_normed, axis=-1, keepdims=True)
        - normed * jnp.mean(grad_normed * normed, axis=-1, keepdims=True)
    )


def gelu_parts(inner):
    cdf_value = 0.5 * (1.0 + lax.erf(inner * 0.7071067811865476))
    slope = cdf_value + inner * jnp.exp(-0.5 * inner * inner) * 0.3989422804014327
    return (cdf_value, slope)


def masked_scores(query, keys, seg_row):
    scores = jnp.einsum("qhd,khd->hqk", query, keys, preferred_element_type=jnp.float32) * HD ** (
        -0.5
    )
    same = seg_row[:, None] == seg_row[None, :]
    return jnp.where(same[None], scores, -1e30)


def attend(item):
    query, keys, values, seg_row = item
    scores = masked_scores(query, keys, seg_row)
    row_max = jnp.max(scores, axis=2, keepdims=True)
    exp_scores = jnp.exp(scores - row_max)
    row_sum = jnp.sum(exp_scores, axis=2, keepdims=True)
    attn_prob = (exp_scores / row_sum).astype(jnp.bfloat16)
    context = jnp.einsum("hqk,khd->qhd", attn_prob, values, preferred_element_type=jnp.float32)
    return (context.astype(jnp.bfloat16), row_max[:, :, 0] + jnp.log(row_sum[:, :, 0]))


def attend_back(item):
    query, keys, values, seg_row, log_total, grad_ctx = item
    attn_prob = jnp.exp(masked_scores(query, keys, seg_row) - log_total[:, :, None])
    grad_values = jnp.einsum(
        "hqk,qhd->khd", attn_prob.astype(jnp.bfloat16), grad_ctx, preferred_element_type=jnp.float32
    )
    grad_prob = jnp.einsum("qhd,khd->hqk", grad_ctx, values, preferred_element_type=jnp.float32)
    grad_scores = attn_prob * (grad_prob - jnp.sum(attn_prob * grad_prob, axis=2, keepdims=True))
    grad_scores = grad_scores.astype(jnp.bfloat16)
    grad_query = jnp.einsum(
        "hqk,khd->qhd", grad_scores, keys, preferred_element_type=jnp.float32
    ) * HD ** (-0.5)
    grad_keys = jnp.einsum(
        "hqk,qhd->khd", grad_scores, query, preferred_element_type=jnp.float32
    ) * HD ** (-0.5)
    return (
        grad_query.astype(jnp.bfloat16),
        grad_keys.astype(jnp.bfloat16),
        grad_values.astype(jnp.bfloat16),
    )


def xor_pairs(count, bit):
    return [(i, i ^ bit) for i in range(count)]


def place(parts, spots, axis):
    shape = list(parts[0].shape)
    shape.insert(axis, len(parts))
    out = jnp.zeros(shape, parts[0].dtype)
    for part, spot in zip(parts, spots):
        out = lax.dynamic_update_index_in_dim(out, part, spot, axis)
    return out


def swap(value, axis_name, count, bit):
    return lax.ppermute(value, axis_name, xor_pairs(count, bit))


def join(value, axis_name, count, bit, axis):
    other = swap(value, axis_name, count, bit)
    own_bit = (lax.axis_index(axis_name) // bit) % 2
    return place([value, other], [own_bit, 1 - own_bit], axis)


def gather_depth(value, depth):
    if depth != 4:
        return lax.all_gather(value, "fsdp", axis=0)
    z = lax.axis_index("fsdp")
    parts = [value] + [swap(value, "fsdp", depth, s) for s in range(1, depth)]
    return place(parts, [z ^ s for s in range(depth)], 0)


def sum_depth(value, depth):
    if depth != 4:
        return lax.psum_scatter(value, "fsdp", scatter_dimension=0).astype(jnp.float32)
    z = lax.axis_index("fsdp")
    pick = lambda s: lax.dynamic_index_in_dim(value, z ^ s, 0, keepdims=False)
    total = pick(0).astype(jnp.float32)
    for s in range(1, depth):
        total = total + swap(pick(s), "fsdp", depth, s).astype(jnp.float32)
    return total


def halve(value, axis_name, count, bit, axis):
    own_bit = (lax.axis_index(axis_name) // bit) % 2
    mine = lax.dynamic_index_in_dim(value, own_bit, axis, keepdims=False)
    sent = lax.dynamic_index_in_dim(value, 1 - own_bit, axis, keepdims=False).astype(jnp.bfloat16)
    got = swap(sent, axis_name, count, bit)
    return (mine.astype(jnp.float32) + got.astype(jnp.float32)).astype(jnp.bfloat16)


def both(value, axis_name, count, bit):
    low = value.astype(jnp.bfloat16)
    got = swap(low, axis_name, count, bit)
    return (low.astype(jnp.float32) + got.astype(jnp.float32)).astype(jnp.bfloat16)


def forward_rows(tok, seg_all, weights):
    (
        w_query,
        b_query,
        w_key,
        w_value,
        b_value,
        w_out,
        b_out,
        gain_attn,
        shift_attn,
        w_inner,
        b_inner,
        w_outer,
        b_outer,
        gain_ffn,
        shift_ffn,
    ) = weights
    row_count, seq_len, model_dim = tok.shape
    tok_flat = tok.reshape(row_count * seq_len, model_dim)
    head_shape = (row_count, seq_len, H, HD)
    query = (plain_dot(tok_flat, w_query) + b_query).astype(jnp.bfloat16).reshape(head_shape)
    keys = plain_dot(tok_flat, w_key).astype(jnp.bfloat16).reshape(head_shape)
    values = (plain_dot(tok_flat, w_value) + b_value).astype(jnp.bfloat16).reshape(head_shape)
    context, log_total = lax.map(attend, (query, keys, values, seg_all))
    context = context.reshape(row_count * seq_len, model_dim)
    normed_attn, inv_attn = normalize(
        tok_flat.astype(jnp.float32) + plain_dot(context, w_out) + b_out
    )
    mid_state = normed_attn * gain_attn + shift_attn
    mid_low = mid_state.astype(jnp.bfloat16)
    inner = plain_dot(mid_low, w_inner) + b_inner
    cdf_value, slope = gelu_parts(inner)
    activ = (inner * cdf_value).astype(jnp.bfloat16)
    normed_ffn, inv_ffn = normalize(mid_state + plain_dot(activ, w_outer) + b_outer)
    final = normed_ffn * gain_ffn + shift_ffn
    saved = (
        query,
        keys,
        values,
        log_total,
        context,
        normed_attn,
        inv_attn,
        mid_low,
        inner,
        activ,
        normed_ffn,
        inv_ffn,
    )
    return (final, saved)


def loss_grad(pooled_low, labels, twins, groups, depth):
    own_count, model_dim = pooled_low.shape
    half_count = labels.shape[0]
    same = pooled_low
    if groups == 4:
        same = join(same, "dp", groups, 1, 0)
        same = join(same, "dp", groups, 2, 0)
        same = gather_depth(same, depth)
        same = same.reshape(depth, groups, own_count, model_dim).swapaxes(0, 1)
        same = same.reshape(half_count, model_dim)
    else:
        same = lax.all_gather(same, ("dp", "fsdp"), axis=0, tiled=True)
    other = swap(same, "twin", twins, 1)
    twin_side = lax.axis_index("twin")
    first = lax.axis_index(("dp", "fsdp")) * own_count
    own_f = pooled_low.astype(jnp.float32)
    same_f = same.astype(jnp.float32)
    other_f = other.astype(jnp.float32)
    inv_own = lax.rsqrt(jnp.sum(own_f * own_f, axis=1) + pool_eps)
    inv_same = lax.rsqrt(jnp.sum(same_f * same_f, axis=1) + pool_eps)
    inv_other = lax.rsqrt(jnp.sum(other_f * other_f, axis=1) + pool_eps)
    similar = sim_scale * back_dot(same, other) * inv_same[:, None] * inv_other[None, :]
    col_max = jnp.max(similar, axis=0, keepdims=True)
    col_log = col_max[0] + jnp.log(jnp.sum(jnp.exp(similar - col_max), axis=0))
    own_sim = lax.dynamic_slice_in_dim(similar, first, own_count, 0)
    row_max = jnp.max(own_sim, axis=1, keepdims=True)
    row_log = row_max[:, 0] + jnp.log(jnp.sum(jnp.exp(own_sim - row_max), axis=1))
    col_index = jnp.arange(half_count, dtype=jnp.int32)
    own_labels = lax.dynamic_slice_in_dim(labels, first, own_count, 0)
    own_index = first + jnp.arange(own_count, dtype=jnp.int32)
    target = jnp.where(
        twin_side == 0,
        col_index[None, :] == own_labels[:, None],
        labels[None, :] == own_index[:, None],
    ).astype(jnp.float32)
    grad_sim = (
        jnp.exp(own_sim - row_log[:, None]) + jnp.exp(own_sim - col_log[None, :]) - 2.0 * target
    )
    grad_raw = sim_scale * grad_sim * inv_own[:, None] * inv_other[None, :]
    return (
        jnp.dot(grad_raw, other_f, precision=lax.Precision.HIGHEST)
        - (jnp.sum(grad_sim * own_sim, axis=1) * inv_own * inv_own)[:, None] * own_f
    )


def per_device(
    sizes,
    tokens,
    w_query,
    b_query,
    w_key,
    w_value,
    b_value,
    w_out,
    b_out,
    gain_attn,
    shift_attn,
    w_inner,
    b_inner,
    w_outer,
    b_outer,
    gain_ffn,
    shift_ffn,
    lengths,
    labels,
):
    twins, groups, depth = sizes
    row_total, seq_len, model_dim = tokens.shape
    token_count = row_total * seq_len
    shard = w_query.shape[0]
    half = shard // 2
    inner_dim = w_inner.shape[1]
    twin = lax.axis_index("twin")
    group = lax.axis_index("dp")
    eighth = twin * 4 + group

    square = jnp.stack([w_query, w_key, w_value, w_out]).reshape(8, half, model_dim)
    piece_a = lax.dynamic_index_in_dim(square, eighth, 0, keepdims=False)
    piece_b = lax.dynamic_slice(
        w_inner, ((eighth % 2) * half, (eighth // 2) * model_dim), (half, model_dim)
    )
    piece_c = lax.dynamic_slice_in_dim(w_outer, eighth * half, half, 0)
    vectors = jnp.concatenate(
        [b_query, b_value, b_out, gain_attn, shift_attn, b_outer, gain_ffn, shift_ffn, b_inner]
    )
    vec_size = vectors.shape[0]
    vec_rows = -(-vec_size // model_dim)
    vec_block = jnp.pad(vectors, (0, vec_rows * model_dim - vec_size)).reshape(vec_rows, model_dim)
    deep_a = gather_depth(jnp.concatenate([piece_a, vec_block]), depth)
    vec_all = deep_a[:, half:].reshape(depth, vec_rows * model_dim)
    full = deep_a[:, :half]
    full = join(full, "dp", groups, 1, 1)
    full = join(full, "dp", groups, 2, 0)
    full = join(full, "twin", twins, 1, 0)
    full = full.reshape(4, model_dim, model_dim)
    wide = gather_depth(piece_b, depth)
    wide = join(wide, "dp", groups, 2, 2)
    wide = wide.reshape(depth, half, 2 * model_dim)
    wide = join(wide, "dp", groups, 1, 1)
    wide = wide.reshape(model_dim, 2 * model_dim)
    wide = join(wide, "twin", twins, 1, 1).reshape(model_dim, inner_dim)
    tall = gather_depth(piece_c, depth)
    tall = join(tall, "dp", groups, 1, 1)
    tall = join(tall, "dp", groups, 2, 1)
    tall = join(tall, "twin", twins, 1, 1).reshape(inner_dim, model_dim)
    small = vec_all[:, : 8 * shard].reshape(depth, 8, shard).swapaxes(0, 1).reshape(8, model_dim)
    full_b_inner = vec_all[:, 8 * shard : vec_size].reshape(inner_dim)
    weights = (
        full[0], small[0], full[1], full[2], small[1], full[3], small[2], small[3], small[4],
        wide, full_b_inner, tall, small[5], small[6], small[7],
    )

    seg_all = segment_ids(lengths, seq_len)
    member = (seg_all[:, None, :] == jnp.arange(SEG, dtype=jnp.int32)[None, :, None]).astype(
        jnp.float32
    )
    counts = lengths[:, :SEG].astype(jnp.float32)
    final, saved = forward_rows(tokens, seg_all, weights)
    output = final.astype(jnp.bfloat16).reshape(row_total, seq_len, model_dim)
    pooled_f = (
        jnp.einsum(
            "rst,rtd->rsd",
            member,
            final.reshape(row_total, seq_len, model_dim),
            precision=lax.Precision.HIGHEST,
        )
        / counts[:, :, None]
    )
    pooled_low = pooled_f.reshape(row_total * SEG, model_dim).astype(jnp.bfloat16)
    grad_pooled = loss_grad(pooled_low, labels, twins, groups, depth)
    grad_scaled = grad_pooled.reshape(row_total, SEG, model_dim) / counts[:, :, None]
    grad_final = jnp.einsum(
        "rst,rsd->rtd", member, grad_scaled, precision=lax.Precision.HIGHEST
    ).reshape(token_count, model_dim)

    (
        query,
        keys,
        values,
        log_total,
        context,
        normed_attn,
        inv_attn,
        mid_low,
        inner,
        activ,
        normed_ffn,
        inv_ffn,
    ) = saved
    tok_flat = tokens.reshape(token_count, model_dim)
    f_w_query, _, f_w_key, f_w_value, _, f_w_out, _, f_gain_attn, _, _, _, _, _, f_gain_ffn, _ = weights
    grad_gain_ffn = jnp.sum(grad_final * normed_ffn, axis=0)
    grad_shift_ffn = jnp.sum(grad_final, axis=0)
    grad_h2 = norm_back(grad_final * f_gain_ffn, normed_ffn, inv_ffn)
    grad_branch = grad_h2.astype(jnp.bfloat16)
    grad_tall = cross_dot(activ, grad_branch).reshape(depth, 2, 2, 2, half, model_dim)
    grad_tall = halve(grad_tall, "twin", twins, 1, 1)
    grad_tall = halve(grad_tall, "dp", groups, 1, 2)
    grad_tall = halve(grad_tall, "dp", groups, 2, 1)
    done_c = sum_depth(grad_tall, depth)
    grad_b_outer = jnp.sum(grad_branch, axis=0, dtype=jnp.float32)
    _, slope = gelu_parts(inner)
    grad_inner = (back_dot(grad_branch, tall) * slope).astype(jnp.bfloat16)
    grad_wide = cross_dot(mid_low, grad_inner).reshape(depth, 2, half, 2, 2 * model_dim)
    grad_wide = halve(grad_wide, "twin", twins, 1, 3).reshape(depth, 2, half, 2, model_dim)
    grad_wide = halve(grad_wide, "dp", groups, 2, 3)
    grad_wide = halve(grad_wide, "dp", groups, 1, 1)
    done_b = sum_depth(grad_wide, depth)
    grad_b_inner = jnp.sum(grad_inner, axis=0, dtype=jnp.float32)
    grad_mid = grad_h2 + back_dot(grad_inner, wide)
    grad_gain_attn = jnp.sum(grad_mid * normed_attn, axis=0)
    grad_shift_attn = jnp.sum(grad_mid, axis=0)
    grad_h1 = norm_back(grad_mid * f_gain_attn, normed_attn, inv_attn)
    grad_attn = grad_h1.astype(jnp.bfloat16)
    grad_w_out = cross_dot(context, grad_attn)
    grad_b_out = jnp.sum(grad_attn, axis=0, dtype=jnp.float32)
    grad_ctx = back_dot(grad_attn, f_w_out).astype(jnp.bfloat16).reshape(row_total, seq_len, H, HD)
    grad_query, grad_keys, grad_values = lax.map(
        attend_back, (query, keys, values, seg_all, log_total, grad_ctx)
    )
    flat_shape = (token_count, model_dim)
    grad_query = grad_query.reshape(flat_shape)
    grad_keys = grad_keys.reshape(flat_shape)
    grad_values = grad_values.reshape(flat_shape)
    grad_w_query = cross_dot(tok_flat, grad_query)
    grad_b_query = jnp.sum(grad_query, axis=0, dtype=jnp.float32)
    grad_w_key = cross_dot(tok_flat, grad_keys)
    grad_w_value = cross_dot(tok_flat, grad_values)
    grad_b_value = jnp.sum(grad_values, axis=0, dtype=jnp.float32)
    grad_tok = (
        grad_h1
        + back_dot(grad_query, f_w_query)
        + back_dot(grad_keys, f_w_key)
        + back_dot(grad_values, f_w_value)
    )
    grad_tokens = grad_tok.astype(jnp.bfloat16).reshape(row_total, seq_len, model_dim)

    grad_square = jnp.stack([grad_w_query, grad_w_key, grad_w_value, grad_w_out]).reshape(
        2, 2, depth, 2, half, model_dim
    )
    vec_grads = jnp.stack(
        [
            grad_b_query,
            grad_b_value,
            grad_b_out,
            grad_gain_attn,
            grad_shift_attn,
            grad_b_outer,
            grad_gain_ffn,
            grad_shift_ffn,
        ]
    )
    vec_grads = vec_grads.reshape(8, depth, shard).swapaxes(0, 1).reshape(depth, 8 * shard)
    vec_grads = jnp.concatenate([vec_grads, grad_b_inner.reshape(depth, 4 * shard)], axis=1)
    vec_grads = jnp.pad(vec_grads, ((0, 0), (0, vec_rows * model_dim - vec_size)))
    vec_grads = both(vec_grads, "twin", twins, 1)
    vec_grads = both(vec_grads, "dp", groups, 1)
    vec_grads = both(vec_grads, "dp", groups, 2)
    grad_square = halve(grad_square, "twin", twins, 1, 0)
    grad_square = halve(grad_square, "dp", groups, 1, 2)
    grad_square = halve(grad_square, "dp", groups, 2, 0)
    last = jnp.concatenate([grad_square, vec_grads.reshape(depth, vec_rows, model_dim)], axis=1)
    last = sum_depth(last, depth)
    vec_done = last[half:].reshape(vec_rows * model_dim)
    pieces = jnp.stack([last[:half], done_b, done_c]).astype(jnp.bfloat16)
    pieces = join(pieces, "dp", groups, 1, 1)
    pieces = join(pieces, "dp", groups, 2, 1)
    pieces = join(pieces, "twin", twins, 1, 1)
    pieces = pieces.astype(jnp.float32)
    out_square = pieces[0].reshape(4, shard, model_dim)
    out_wide = pieces[1].reshape(4, shard, model_dim).swapaxes(0, 1).reshape(shard, inner_dim)
    out_tall = pieces[2].reshape(4 * shard, model_dim)
    vec = vec_done[: 8 * shard].reshape(8, shard)
    return (
        output,
        grad_tokens,
        out_square[0],
        vec[0],
        out_square[1],
        out_square[2],
        vec[1],
        out_square[3],
        vec[2],
        vec[3],
        vec[4],
        out_wide,
        vec_done[8 * shard : vec_size],
        out_tall,
        vec[5],
        vec[6],
        vec[7],
    )


def solution(mesh):
    placed = (
        P(("twin", "dp", "fsdp"), None, None),
        P("fsdp", None),
        P("fsdp"),
        P("fsdp", None),
        P("fsdp", None),
        P("fsdp"),
        P("fsdp", None),
        P("fsdp"),
        P("fsdp"),
        P("fsdp"),
        P("fsdp", None),
        P("fsdp"),
        P("fsdp", None),
        P("fsdp"),
        P("fsdp"),
        P("fsdp"),
        P(("twin", "dp", "fsdp"), None),
        P(),
    )
    sizes = (mesh.shape["twin"], mesh.shape["dp"], mesh.shape["fsdp"])
    return jax.shard_map(
        functools.partial(per_device, sizes),
        mesh=mesh,
        in_specs=placed,
        out_specs=(
            P(("twin", "dp", "fsdp"), None, None),
            P(("twin", "dp", "fsdp"), None, None),
            P("fsdp", None),
            P("fsdp"),
            P("fsdp", None),
            P("fsdp", None),
            P("fsdp"),
            P("fsdp", None),
            P("fsdp"),
            P("fsdp"),
            P("fsdp"),
            P("fsdp", None),
            P("fsdp"),
            P("fsdp", None),
            P("fsdp"),
            P("fsdp"),
            P("fsdp"),
        ),
        check_vma=False,
    )
```

```python
import jax
import jax.numpy as jnp
from jax import lax
from jax.experimental import pallas as pl
from jax.experimental.pallas import tpu as pltpu
from jax.sharding import PartitionSpec as P

H = 12
HD = 64
SEG = 8
MB = 2
TQ = 128


norm_eps = 1e-12
pool_eps = 1e-06
sim_scale = 20.0


def cross_dot(left, right):
    return lax.dot_general(
        left, right, (((0,), (0,)), ((), ())), preferred_element_type=jnp.float32
    )


def back_dot(left, right):
    return lax.dot_general(
        left, right, (((1,), (1,)), ((), ())), preferred_element_type=jnp.float32
    )


def plain_dot(left, right):
    return jnp.dot(left, right, preferred_element_type=jnp.float32)


def segment_ids(lengths, seq_len):
    ends = jnp.cumsum(lengths, axis=1, dtype=jnp.int32)
    position = jnp.arange(seq_len, dtype=jnp.int32)
    return jnp.sum((position[None, :, None] >= ends[:, None, :]).astype(jnp.int32), axis=2)


def normalize(hidden):
    centred = hidden - jnp.mean(hidden, axis=-1, keepdims=True)
    inv_dev = lax.rsqrt(jnp.mean(centred * centred, axis=-1, keepdims=True) + norm_eps)
    return (centred * inv_dev, inv_dev)


def norm_back(grad_normed, normed, inv_dev):
    return inv_dev * (
        grad_normed
        - jnp.mean(grad_normed, axis=-1, keepdims=True)
        - normed * jnp.mean(grad_normed * normed, axis=-1, keepdims=True)
    )


def gelu_parts(inner):
    cdf_value = 0.5 * (1.0 + lax.erf(inner * 0.7071067811865476))
    slope = cdf_value + inner * jnp.exp(-0.5 * inner * inner) * 0.3989422804014327
    return (cdf_value, slope)


def key_span(tile, seq_len):
    return max(0, (tile - 1) * TQ), min(seq_len, (tile + 2) * TQ)


def split_heads(block):
    lane = lax.broadcasted_iota(jnp.int32, block.shape, 1)
    zero = jnp.zeros_like(block)
    return jnp.concatenate(
        [jnp.where(lane < HD, block, zero), jnp.where(lane < HD, zero, block)], axis=0
    )


def merge_heads(double):
    count = double.shape[0] // 2
    lane = lax.broadcasted_iota(jnp.int32, (count, double.shape[1]), 1)
    return jnp.where(lane < HD, double[:count], double[count:])


def fill_bias(seg_col_ref, seg_row_ref, bias_ref, seq_len):
    for tile in range(seq_len // TQ):
        low, high = key_span(tile, seq_len)
        same = seg_col_ref[low:high, :] == seg_row_ref[:, tile * TQ : (tile + 1) * TQ]
        bias_ref[tile, : high - low, :] = jnp.where(same, 0.0, -1e30)


def attend_kernel(seg_col_ref, seg_row_ref, tok_ref, qkv_ref, ctx_ref, log_ref, bias_ref):
    seq_len = tok_ref.shape[0]

    @pl.when(pl.program_id(1) == 0)
    def _():
        fill_bias(seg_col_ref, seg_row_ref, bias_ref, seq_len)

    ctx_ref[0] = tok_ref[...]
    for tile in range(seq_len // TQ):
        low, high = key_span(tile, seq_len)
        rows = slice(tile * TQ, (tile + 1) * TQ)
        query = split_heads(qkv_ref[0, rows, :] * jnp.bfloat16(HD**-0.5))
        bias = bias_ref[tile, : high - low, :]
        scores = back_dot(qkv_ref[1, low:high, :], query) + jnp.concatenate([bias, bias], axis=1)
        top = jnp.max(scores, axis=0, keepdims=True)
        exp_scores = jnp.exp(scores - top)
        row_sum = jnp.sum(exp_scores, axis=0, keepdims=True)
        prob = (exp_scores * (1.0 / row_sum)).astype(jnp.bfloat16)
        context = cross_dot(prob, qkv_ref[2, low:high, :])
        ctx_ref[1, rows, :] = merge_heads(context).astype(jnp.bfloat16)
        log_ref[0, 0, tile : tile + 1, :] = top + jnp.log(row_sum)


def attend_back_kernel(
    seg_col_ref, seg_row_ref, qkv_ref, grad_ref, log_ref, attn_ref, out_ref, bias_ref, key_acc, val_acc
):
    seq_len = attn_ref.shape[0]

    @pl.when(pl.program_id(1) == 0)
    def _():
        fill_bias(seg_col_ref, seg_row_ref, bias_ref, seq_len)

    key_acc[...] = jnp.zeros_like(key_acc)
    val_acc[...] = jnp.zeros_like(val_acc)
    out_ref[3] = attn_ref[...]
    for tile in range(seq_len // TQ):
        low, high = key_span(tile, seq_len)
        rows = slice(tile * TQ, (tile + 1) * TQ)
        query = split_heads(qkv_ref[0, rows, :] * jnp.bfloat16(HD**-0.5))
        grad = split_heads(grad_ref[rows, :])
        bias = bias_ref[tile, : high - low, :]
        keys = qkv_ref[1, low:high, :]
        scores = back_dot(keys, query) + jnp.concatenate([bias, bias], axis=1)
        prob = jnp.exp(scores - log_ref[0, 0, tile : tile + 1, :])
        grad_prob = back_dot(qkv_ref[2, low:high, :], grad)
        total = jnp.sum(prob * grad_prob, axis=0, keepdims=True)
        grad_scores = (prob * (grad_prob - total)).astype(jnp.bfloat16)
        val_acc[low:high, :] += plain_dot(prob.astype(jnp.bfloat16), grad)
        key_acc[low:high, :] += plain_dot(grad_scores, query)
        grad_query = merge_heads(cross_dot(grad_scores, keys))
        out_ref[0, rows, :] = (grad_query * HD**-0.5).astype(jnp.bfloat16)
    out_ref[1] = key_acc[...].astype(jnp.bfloat16)
    out_ref[2] = val_acc[...].astype(jnp.bfloat16)


def attend(seg_all, tok_flat, qkv):
    row_count, seq_len = seg_all.shape
    token_count, model_dim = tok_flat.shape
    pairs = model_dim // (2 * HD)
    tiles = seq_len // TQ
    return pl.pallas_call(
        attend_kernel,
        grid=(row_count, pairs),
        in_specs=[
            pl.BlockSpec((None, seq_len, 1), lambda r, p: (r, 0, 0)),
            pl.BlockSpec((None, 1, seq_len), lambda r, p: (r, 0, 0)),
            pl.BlockSpec((seq_len, 2 * HD), lambda r, p: (r, p)),
            pl.BlockSpec((3, seq_len, 2 * HD), lambda r, p: (0, r, p)),
        ],
        out_specs=[
            pl.BlockSpec((2, seq_len, 2 * HD), lambda r, p: (0, r, p)),
            pl.BlockSpec((1, 1, tiles, 2 * TQ), lambda r, p: (r, p, 0, 0)),
        ],
        out_shape=[
            jax.ShapeDtypeStruct((2, token_count, model_dim), jnp.bfloat16),
            jax.ShapeDtypeStruct((row_count, pairs, tiles, 2 * TQ), jnp.float32),
        ],
        scratch_shapes=[pltpu.VMEM((tiles, 3 * TQ, TQ), jnp.float32)],
        cost_estimate=pl.CostEstimate(
            flops=4 * token_count * 3 * TQ * model_dim * 2,
            bytes_accessed=token_count * model_dim * 14,
            transcendentals=token_count * 3 * TQ * 2 * pairs,
        ),
        name="attend",
    )(seg_all[:, :, None], seg_all[:, None, :], tok_flat, qkv)


def attend_back(seg_all, qkv, grad_ctx, log_total, grad_attn):
    row_count, seq_len = seg_all.shape
    token_count, model_dim = grad_ctx.shape
    pairs = model_dim // (2 * HD)
    tiles = seq_len // TQ
    flat = pl.BlockSpec((seq_len, 2 * HD), lambda r, p: (r, p))
    return pl.pallas_call(
        attend_back_kernel,
        grid=(row_count, pairs),
        in_specs=[
            pl.BlockSpec((None, seq_len, 1), lambda r, p: (r, 0, 0)),
            pl.BlockSpec((None, 1, seq_len), lambda r, p: (r, 0, 0)),
            pl.BlockSpec((3, seq_len, 2 * HD), lambda r, p: (0, r, p)),
            flat,
            pl.BlockSpec((1, 1, tiles, 2 * TQ), lambda r, p: (r, p, 0, 0)),
            flat,
        ],
        out_specs=pl.BlockSpec((4, seq_len, 2 * HD), lambda r, p: (0, r, p)),
        out_shape=jax.ShapeDtypeStruct((4, token_count, model_dim), jnp.bfloat16),
        scratch_shapes=[
            pltpu.VMEM((tiles, 3 * TQ, TQ), jnp.float32),
            pltpu.VMEM((seq_len, 2 * HD), jnp.float32),
            pltpu.VMEM((seq_len, 2 * HD), jnp.float32),
        ],
        cost_estimate=pl.CostEstimate(
            flops=10 * token_count * 3 * TQ * model_dim * 2,
            bytes_accessed=token_count * model_dim * 20,
            transcendentals=token_count * 3 * TQ * 2 * pairs,
        ),
        name="attend_back",
    )(seg_all[:, :, None], seg_all[:, None, :], qkv, grad_ctx, log_total, grad_attn)


def swap(value, axis_name, bit):
    count = 2 if axis_name == "twin" else 4
    return lax.ppermute(value, axis_name, [(i, i ^ bit) for i in range(count)])


def gather_eighths(piece):
    own = jnp.stack([swap(piece, "fsdp", s) for s in (1, 2, 3)])
    beside = swap(own, "dp", 1)
    above = swap(own, "dp", 2)
    if piece.shape[0] == 1:
        corner = swap(beside, "dp", 2)
    else:
        corner = jnp.concatenate(
            [swap(beside[:, :1], "dp", 2), swap(above[:, 1:], "dp", 1)], axis=1
        )
    near = jnp.stack([own, beside, above, corner])
    return near, swap(near, "twin", 1)


def assemble_wide_kernel(place_ref, *refs):
    step = pl.program_id(0)
    out_ref = refs[-1]
    count = len(refs) - 3
    near_ref, far_ref = refs[count], refs[count + 1]
    model_dim = near_ref.shape[-1]
    half = near_ref.shape[-2]

    @pl.when(step == 0)
    def _():
        if count == 1:
            out_ref[...] = refs[0][...]
        else:
            for index in range(count):
                out_ref[:, index * model_dim : (index + 1) * model_dim] = refs[index][...]

    @pl.when(step > 0)
    def _():
        for index in range(8):
            spot = place_ref[1] ^ index
            source = near_ref if index < 4 else far_ref
            row = pl.multiple_of((spot % 2) * half, half)
            column = pl.multiple_of((spot // 2) * model_dim, model_dim)
            out_ref[pl.ds(row, half), pl.ds(column, model_dim)] = source[index % 4]


def assemble_tall_kernel(place_ref, shard_ref, near_ref, far_ref, out_ref):
    step = pl.program_id(0)
    half = near_ref.shape[-2]

    @pl.when(step == 0)
    def _():
        out_ref[...] = shard_ref[...]

    @pl.when(step > 0)
    def _():
        for index in range(8):
            source = near_ref if index < 4 else far_ref
            row = pl.multiple_of((place_ref[1] ^ index) * half, half)
            out_ref[pl.ds(row, half), :] = source[index % 4]


def assemble(kernel, place, shards, near, far, part, name):
    rows = shards[0].shape[0]
    columns = sum(shard.shape[1] for shard in shards)
    half, model_dim = near.shape[-2:]
    gathered = pl.BlockSpec(
        (4, None, None, half, model_dim),
        lambda s, place: (0, jnp.maximum(s - 1, 0), part, 0, 0),
    )
    return pl.pallas_call(
        kernel,
        grid_spec=pltpu.PrefetchScalarGridSpec(
            num_scalar_prefetch=1,
            grid=(4,),
            in_specs=[pl.BlockSpec(shard.shape, lambda s, place: (0, 0)) for shard in shards]
            + [gathered, gathered],
            out_specs=pl.BlockSpec((rows, columns), lambda s, place: (place[0] ^ s, 0)),
        ),
        out_shape=jax.ShapeDtypeStruct((4 * rows, columns), jnp.bfloat16),
        cost_estimate=pl.CostEstimate(
            flops=0, bytes_accessed=16 * rows * columns, transcendentals=0
        ),
        name=name,
    )(place, *shards, near, far)


def project_kernel(tok_ref, weight_ref, bias_ref, out_ref):
    out_ref[...] = (plain_dot(tok_ref[...], weight_ref[...]) + bias_ref[0]).astype(jnp.bfloat16)


def project(tok_flat, square, biases):
    token_count, model_dim = tok_flat.shape
    return pl.pallas_call(
        project_kernel,
        grid=(3,),
        in_specs=[
            pl.BlockSpec((token_count, model_dim), lambda m: (0, 0)),
            pl.BlockSpec((model_dim, model_dim), lambda m: (0, m)),
            pl.BlockSpec((1, 1, model_dim), lambda m: (m, 0, 0)),
        ],
        out_specs=pl.BlockSpec((None, token_count, model_dim), lambda m: (m, 0, 0)),
        out_shape=jax.ShapeDtypeStruct((3, token_count, model_dim), jnp.bfloat16),
        cost_estimate=pl.CostEstimate(
            flops=6 * token_count * model_dim**2,
            bytes_accessed=8 * token_count * model_dim,
            transcendentals=0,
        ),
        name="project",
    )(tok_flat, square, biases)


def project_back_kernel(grad_ref, weight_ref, base_ref, out_ref, acc_ref):
    step = pl.program_id(0)

    @pl.when(step == 0)
    def _():
        acc_ref[...] = base_ref[...]

    acc_ref[...] += back_dot(grad_ref[...], weight_ref[...])

    @pl.when(step == 2)
    def _():
        out_ref[...] = acc_ref[...].astype(jnp.bfloat16)


def project_back(grads, square, base):
    _, token_count, model_dim = grads.shape
    return pl.pallas_call(
        project_back_kernel,
        grid=(3,),
        in_specs=[
            pl.BlockSpec((None, token_count, model_dim), lambda m: (m, 0, 0)),
            pl.BlockSpec((model_dim, model_dim), lambda m: (0, m)),
            pl.BlockSpec((token_count, model_dim), lambda m: (0, 0)),
        ],
        out_specs=pl.BlockSpec((token_count, model_dim), lambda m: (0, 0)),
        out_shape=jax.ShapeDtypeStruct((token_count, model_dim), jnp.bfloat16),
        scratch_shapes=[pltpu.VMEM((token_count, model_dim), jnp.float32)],
        cost_estimate=pl.CostEstimate(
            flops=6 * token_count * model_dim**2,
            bytes_accessed=8 * token_count * model_dim,
            transcendentals=0,
        ),
        name="project_back",
    )(grads, square, base)


def weight_grad_kernel(place_ref, left_ref, right_ref, out_ref, acc_ref):
    acc_ref[...] = cross_dot(left_ref[...], right_ref[...])
    half = out_ref.shape[-2]
    for x in range(2):
        for z in range(4):
            row = pl.multiple_of(
                ((place_ref[0] ^ z) * 2 + ((place_ref[1] ^ x) % 2)) * half, half
            )
            out_ref[x, z] = acc_ref[pl.ds(row, half), :].astype(jnp.bfloat16)


def weight_grad_tall_kernel(place_ref, left_ref, right_ref, out_ref, acc_ref):
    acc_ref[...] = cross_dot(left_ref[...], right_ref[...])
    half = out_ref.shape[-2]
    for index in range(4):
        row = pl.multiple_of(((place_ref[1] ^ index) % 4) * half, half)
        out_ref[index // 2, index % 2] = acc_ref[pl.ds(row, half), :].astype(jnp.bfloat16)


def weight_grad(kind, side, place, left, right):
    token_count, model_dim = left.shape[-2], 768 if kind is None else right.shape[-1]
    model_dim = left.shape[-1] if kind != "tall" else right.shape[-1]
    half = model_dim // 8
    block = lambda y, place: (place[1] // 2) ^ (2 * side + y)
    if kind == "square":
        left_spec = pl.BlockSpec(
            (None, token_count, model_dim), lambda y, place: (block(y, place) // 3, 0, 0)
        )
        right_spec = pl.BlockSpec(
            (None, token_count, model_dim), lambda y, place: (block(y, place), 0, 0)
        )
    elif kind == "wide":
        left_spec = pl.BlockSpec((token_count, model_dim), lambda y, place: (0, 0))
        right_spec = pl.BlockSpec((token_count, model_dim), lambda y, place: (0, block(y, place)))
    if kind == "tall":
        return pl.pallas_call(
            weight_grad_tall_kernel,
            grid_spec=pltpu.PrefetchScalarGridSpec(
                num_scalar_prefetch=1,
                grid=(4,),
                in_specs=[
                    pl.BlockSpec(
                        (token_count, model_dim // 2),
                        lambda z, place: (0, (place[0] ^ z) * 2 + ((place[1] // 4) ^ side)),
                    ),
                    pl.BlockSpec((token_count, model_dim), lambda z, place: (0, 0)),
                ],
                out_specs=pl.BlockSpec(
                    (2, 2, None, half, model_dim), lambda z, place: (0, 0, z, 0, 0)
                ),
                scratch_shapes=[pltpu.VMEM((model_dim // 2, model_dim), jnp.float32)],
            ),
            out_shape=jax.ShapeDtypeStruct((2, 2, 4, half, model_dim), jnp.bfloat16),
            cost_estimate=pl.CostEstimate(
                flops=4 * token_count * model_dim**2,
                bytes_accessed=8 * token_count * model_dim,
                transcendentals=0,
            ),
            name="weight_grad_tall",
        )(place, left, right)
    return pl.pallas_call(
        weight_grad_kernel,
        grid_spec=pltpu.PrefetchScalarGridSpec(
            num_scalar_prefetch=1,
            grid=(2,),
            in_specs=[left_spec, right_spec],
            out_specs=pl.BlockSpec(
                (None, 2, 4, half, model_dim), lambda y, place: (y, 0, 0, 0, 0)
            ),
            scratch_shapes=[pltpu.VMEM((model_dim, model_dim), jnp.float32)],
        ),
        out_shape=jax.ShapeDtypeStruct((2, 2, 4, half, model_dim), jnp.bfloat16),
        cost_estimate=pl.CostEstimate(
            flops=4 * token_count * model_dim**2,
            bytes_accessed=8 * token_count * model_dim,
            transcendentals=0,
        ),
        name="weight_grad_" + kind,
    )(place, left, right)


def add_low(*parts):
    total = parts[0].astype(jnp.float32)
    for part in parts[1:]:
        total = total + part.astype(jnp.float32)
    return total.astype(jnp.bfloat16)


def reduce_dp(mine, got, y_first):
    if y_first:
        other = swap(add_low(mine[1], got[1]), "dp", 2)
        send = add_low(mine[0, 1], got[0, 1], other[1])
        last = swap(send, "dp", 1)
        return add_low(mine[0, 0], got[0, 0], other[0], last)
    other = swap(add_low(mine[:, 1], got[:, 1]), "dp", 1)
    send = add_low(mine[1, 0], got[1, 0], other[1])
    last = swap(send, "dp", 2)
    return add_low(mine[0, 0], got[0, 0], other[0], last)


def reduce_fsdp(value):
    return add_low(value[0], *[swap(value[s], "fsdp", s) for s in (1, 2, 3)])


def gather_back(piece):
    pair = jnp.stack([piece, swap(piece, "dp", 1)])
    quad = jnp.concatenate([pair, swap(pair, "dp", 2)])
    return quad, swap(quad, "twin", 1)


def scatter_out_kernel(place_ref, quad_a, far_a, quad_b, far_b, *outs):
    half, model_dim = quad_a.shape[-2:]
    for index in range(8):
        spot = place_ref[1] ^ index
        pick = lambda near, far: (near if index < 4 else far)[index % 4]
        value = pick(quad_a, far_a).astype(jnp.float32)
        row = pl.multiple_of((spot % 2) * half, half)
        for matrix in range(4):

            @pl.when(spot // 2 == matrix)
            def _():
                outs[matrix][pl.ds(row, half), :] = value

        column = pl.multiple_of((spot // 2) * model_dim, model_dim)
        both = pick(quad_b, far_b)
        outs[4][pl.ds(row, half), pl.ds(column, model_dim)] = both[1].astype(jnp.float32)
        tall_row = pl.multiple_of(spot * half, half)
        outs[5][pl.ds(tall_row, half), :] = both[0].astype(jnp.float32)


def scatter_out(place, gathered_a, gathered_b):
    half, model_dim = gathered_a[0].shape[-2:]
    shard = 2 * half
    whole = pl.BlockSpec(memory_space=pltpu.VMEM)
    shapes = [(shard, model_dim)] * 4 + [(shard, 4 * model_dim), (4 * shard, model_dim)]
    return pl.pallas_call(
        scatter_out_kernel,
        in_specs=[pl.BlockSpec(memory_space=pltpu.SMEM)] + [whole] * 4,
        out_specs=[whole] * 6,
        out_shape=[jax.ShapeDtypeStruct(shape, jnp.float32) for shape in shapes],
        name="scatter_out",
    )(place, *gathered_a, *gathered_b)


def loss_grad(pooled_low, labels):
    own_count, model_dim = pooled_low.shape
    half_count = labels.shape[0]
    same = jnp.stack([pooled_low, swap(pooled_low, "dp", 1)])
    same = jnp.concatenate([same, swap(same, "dp", 2)])
    same = jnp.stack([same] + [swap(same, "fsdp", s) for s in (1, 2, 3)])
    same = same.reshape(half_count, model_dim)
    other = swap(same, "twin", 1)
    twin_side = lax.axis_index("twin")
    group, depth = lax.axis_index("dp"), lax.axis_index("fsdp")
    first = (group * 4 + depth) * own_count
    offset = jnp.arange(4, dtype=jnp.int32)
    numbers = ((offset[None, :] ^ group) * 4 + (offset[:, None] ^ depth)).reshape(16)
    numbers = (
        numbers[:, None] * own_count + jnp.arange(own_count, dtype=jnp.int32)[None, :]
    ).reshape(half_count)
    own_f = pooled_low.astype(jnp.float32)
    same_f = same.astype(jnp.float32)
    other_f = other.astype(jnp.float32)
    inv_own = lax.rsqrt(jnp.sum(own_f * own_f, axis=1) + pool_eps)
    inv_same = lax.rsqrt(jnp.sum(same_f * same_f, axis=1) + pool_eps)
    inv_other = lax.rsqrt(jnp.sum(other_f * other_f, axis=1) + pool_eps)
    similar = sim_scale * back_dot(same, other) * inv_same[:, None] * inv_other[None, :]
    col_max = jnp.max(similar, axis=0, keepdims=True)
    col_log = col_max[0] + jnp.log(jnp.sum(jnp.exp(similar - col_max), axis=0))
    own_sim = similar[:own_count]
    row_max = jnp.max(own_sim, axis=1, keepdims=True)
    row_log = row_max[:, 0] + jnp.log(jnp.sum(jnp.exp(own_sim - row_max), axis=1))
    own_labels = lax.dynamic_slice_in_dim(labels, first, own_count, 0)
    own_index = first + jnp.arange(own_count, dtype=jnp.int32)
    other_labels = labels[numbers]
    target = jnp.where(
        twin_side == 0,
        numbers[None, :] == own_labels[:, None],
        other_labels[None, :] == own_index[:, None],
    ).astype(jnp.float32)
    grad_sim = (
        jnp.exp(own_sim - row_log[:, None]) + jnp.exp(own_sim - col_log[None, :]) - 2.0 * target
    )
    grad_raw = sim_scale * grad_sim * inv_own[:, None] * inv_other[None, :]
    return (
        jnp.dot(grad_raw, other_f, precision=lax.Precision.HIGHEST)
        - (jnp.sum(grad_sim * own_sim, axis=1) * inv_own * inv_own)[:, None] * own_f
    )


def per_device(
    tokens,
    w_query,
    b_query,
    w_key,
    w_value,
    b_value,
    w_out,
    b_out,
    gain_attn,
    shift_attn,
    w_inner,
    b_inner,
    w_outer,
    b_outer,
    gain_ffn,
    shift_ffn,
    lengths,
    labels,
):
    row_total, seq_len, model_dim = tokens.shape
    token_count = row_total * seq_len
    shard = w_query.shape[0]
    half = shard // 2
    inner_dim = w_inner.shape[1]
    eighth = lax.axis_index("twin") * 4 + lax.axis_index("dp")
    depth = lax.axis_index("fsdp")
    place = jnp.stack([depth, eighth]).astype(jnp.int32)
    tok_flat = tokens.reshape(token_count, model_dim)

    stacked = jnp.stack([w_query, w_key, w_value, w_out]).reshape(8, half, model_dim)
    piece_a = lax.dynamic_index_in_dim(stacked, eighth, 0)
    piece_b = lax.dynamic_slice(
        w_inner, ((eighth % 2) * half, (eighth // 2) * model_dim), (half, model_dim)
    )
    piece_c = lax.dynamic_slice_in_dim(w_outer, eighth * half, half, 0)
    near_a, far_a = gather_eighths(piece_a)
    near_b, far_b = gather_eighths(jnp.stack([piece_b, piece_c]))
    vectors = jnp.stack(
        [b_query, b_value, b_out, gain_attn, shift_attn, b_outer, gain_ffn, shift_ffn]
    )
    vectors = jnp.concatenate([vectors.reshape(8 * shard), b_inner])
    around = [vectors] + [swap(vectors, "fsdp", s) for s in (1, 2, 3)]
    ordered = jnp.stack(
        [sum(jnp.where(depth == z ^ s, around[s], 0) for s in range(4)) for z in range(4)]
    ).astype(jnp.float32)
    small = ordered[:, : 8 * shard].reshape(4, 8, shard).swapaxes(0, 1).reshape(8, model_dim)
    full_b_inner = ordered[:, 8 * shard :].reshape(inner_dim)
    b_query, b_value, b_out, gain_attn, shift_attn, b_outer, gain_ffn, shift_ffn = small
    biases = jnp.stack([b_query, jnp.zeros_like(b_query), b_value])[:, None]
    square = assemble(
        assemble_wide_kernel, place, [w_query, w_key, w_value, w_out], near_a, far_a, 0, "assemble_a"
    )
    wide = assemble(assemble_wide_kernel, place, [w_inner], near_b, far_b, 0, "assemble_b")
    tall = assemble(assemble_tall_kernel, place, [w_outer], near_b, far_b, 1, "assemble_c")
    full_w_out = square[:, 3 * model_dim :]

    seg_all = segment_ids(lengths, seq_len)
    member = (seg_all[:, None, :] == jnp.arange(SEG, dtype=jnp.int32)[None, :, None]).astype(
        jnp.float32
    )
    counts = lengths[:, :SEG].astype(jnp.float32)

    qkv = project(tok_flat, square, biases)
    tok_ctx, log_total = attend(seg_all, tok_flat, qkv)
    context = tok_ctx[1]
    normed_attn, inv_attn = normalize(
        tok_flat.astype(jnp.float32) + plain_dot(context, full_w_out) + b_out
    )
    mid_state = normed_attn * gain_attn + shift_attn
    mid_low = mid_state.astype(jnp.bfloat16)
    inner = plain_dot(mid_low, wide) + full_b_inner
    cdf_value, slope = gelu_parts(inner)
    activ = (inner * cdf_value).astype(jnp.bfloat16)
    normed_ffn, inv_ffn = normalize(mid_state + plain_dot(activ, tall) + b_outer)
    final = normed_ffn * gain_ffn + shift_ffn
    output = final.astype(jnp.bfloat16).reshape(row_total, seq_len, model_dim)
    pooled_f = (
        jnp.einsum(
            "rst,rtd->rsd",
            member,
            final.reshape(row_total, seq_len, model_dim),
            precision=lax.Precision.HIGHEST,
        )
        / counts[:, :, None]
    )
    pooled_low = pooled_f.reshape(row_total * SEG, model_dim).astype(jnp.bfloat16)
    grad_pooled = loss_grad(pooled_low, labels)
    grad_scaled = grad_pooled.reshape(row_total, SEG, model_dim) / counts[:, :, None]
    grad_final = jnp.einsum(
        "rst,rsd->rtd", member, grad_scaled, precision=lax.Precision.HIGHEST
    ).reshape(token_count, model_dim)

    grad_gain_ffn = jnp.sum(grad_final * normed_ffn, axis=0)
    grad_shift_ffn = jnp.sum(grad_final, axis=0)
    grad_h2 = norm_back(grad_final * gain_ffn, normed_ffn, inv_ffn)
    grad_branch = grad_h2.astype(jnp.bfloat16)
    sent_c = swap(weight_grad("tall", 1, place, activ, grad_branch), "twin", 1)
    mine_c = weight_grad("tall", 0, place, activ, grad_branch)
    grad_b_outer = jnp.sum(grad_branch, axis=0, dtype=jnp.float32)
    grad_inner = (back_dot(grad_branch, tall) * slope).astype(jnp.bfloat16)
    sent_b = swap(weight_grad("wide", 1, place, mid_low, grad_inner), "twin", 1)
    mine_b = weight_grad("wide", 0, place, mid_low, grad_inner)
    grad_b_inner = jnp.sum(grad_inner, axis=0, dtype=jnp.float32)
    done_c = reduce_dp(mine_c, sent_c, False)
    done_b = reduce_dp(mine_b, sent_b, True)
    done_cb = reduce_fsdp(jnp.stack([done_c, done_b], axis=1))
    back_cb = gather_back(done_cb)

    grad_mid = grad_h2 + back_dot(grad_inner, wide)
    grad_gain_attn = jnp.sum(grad_mid * normed_attn, axis=0)
    grad_shift_attn = jnp.sum(grad_mid, axis=0)
    grad_h1 = norm_back(grad_mid * gain_attn, normed_attn, inv_attn)
    grad_attn = grad_h1.astype(jnp.bfloat16)
    grad_b_out = jnp.sum(grad_attn, axis=0, dtype=jnp.float32)
    grad_ctx = back_dot(grad_attn, full_w_out).astype(jnp.bfloat16)
    grads = attend_back(seg_all, qkv, grad_ctx, log_total, grad_attn)
    sent_a = swap(weight_grad("square", 1, place, tok_ctx, grads), "twin", 1)
    mine_a = weight_grad("square", 0, place, tok_ctx, grads)
    grad_b_query = jnp.sum(grads[0], axis=0, dtype=jnp.float32)
    grad_b_value = jnp.sum(grads[2], axis=0, dtype=jnp.float32)
    grad_tokens = project_back(grads, square, grad_h1).reshape(row_total, seq_len, model_dim)

    vec = jnp.stack(
        [
            grad_b_query,
            grad_b_value,
            grad_b_out,
            grad_gain_attn,
            grad_shift_attn,
            grad_b_outer,
            grad_gain_ffn,
            grad_shift_ffn,
        ]
    )
    vec = jnp.concatenate([vec, grad_b_inner.reshape(4, model_dim)]).astype(jnp.bfloat16)
    for axis_name, bit in (("twin", 1), ("dp", 1), ("dp", 2)):
        vec = add_low(vec, swap(vec, axis_name, bit))
    vec = vec.astype(jnp.float32) + sum(
        swap(vec, "fsdp", s).astype(jnp.float32) for s in (1, 2, 3)
    )
    vec_small = lax.dynamic_slice(vec, (0, depth * shard), (8, shard))
    out_b_inner = lax.dynamic_index_in_dim(vec[8:], depth, 0, keepdims=False)

    done_a = reduce_fsdp(reduce_dp(mine_a, sent_a, True))
    back_a = gather_back(done_a)
    outs = scatter_out(place, back_a, back_cb)
    return (
        output,
        grad_tokens,
        outs[0],
        vec_small[0],
        outs[1],
        outs[2],
        vec_small[1],
        outs[3],
        vec_small[2],
        vec_small[3],
        vec_small[4],
        outs[4],
        out_b_inner,
        outs[5],
        vec_small[5],
        vec_small[6],
        vec_small[7],
    )


def masked_scores(query, keys, seg_row):
    scores = jnp.einsum("qhd,khd->hqk", query, keys, preferred_element_type=jnp.float32) * HD ** (
        -0.5
    )
    same = seg_row[:, None] == seg_row[None, :]
    return jnp.where(same[None], scores, -1e30)


def attend_row(item):
    query, keys, values, seg_row = item
    scores = masked_scores(query, keys, seg_row)
    row_max = jnp.max(scores, axis=2, keepdims=True)
    exp_scores = jnp.exp(scores - row_max)
    row_sum = jnp.sum(exp_scores, axis=2, keepdims=True)
    attn_prob = (exp_scores / row_sum).astype(jnp.bfloat16)
    context = jnp.einsum("hqk,khd->qhd", attn_prob, values, preferred_element_type=jnp.float32)
    return (context.astype(jnp.bfloat16), row_max[:, :, 0] + jnp.log(row_sum[:, :, 0]))


def attend_row_back(item):
    query, keys, values, seg_row, log_total, grad_ctx = item
    attn_prob = jnp.exp(masked_scores(query, keys, seg_row) - log_total[:, :, None])
    grad_values = jnp.einsum(
        "hqk,qhd->khd", attn_prob.astype(jnp.bfloat16), grad_ctx, preferred_element_type=jnp.float32
    )
    grad_prob = jnp.einsum("qhd,khd->hqk", grad_ctx, values, preferred_element_type=jnp.float32)
    grad_scores = attn_prob * (grad_prob - jnp.sum(attn_prob * grad_prob, axis=2, keepdims=True))
    grad_scores = grad_scores.astype(jnp.bfloat16)
    grad_query = jnp.einsum(
        "hqk,khd->qhd", grad_scores, keys, preferred_element_type=jnp.float32
    ) * HD ** (-0.5)
    grad_keys = jnp.einsum(
        "hqk,qhd->khd", grad_scores, query, preferred_element_type=jnp.float32
    ) * HD ** (-0.5)
    return (
        grad_query.astype(jnp.bfloat16),
        grad_keys.astype(jnp.bfloat16),
        grad_values.astype(jnp.bfloat16),
    )


def forward_block(block_tok, seg_block, weights):
    (
        w_query,
        b_query,
        w_key,
        w_value,
        b_value,
        w_out,
        b_out,
        gain_attn,
        shift_attn,
        w_inner,
        b_inner,
        w_outer,
        b_outer,
        gain_ffn,
        shift_ffn,
    ) = weights
    row_count, seq_len, model_dim = block_tok.shape
    tok_flat = block_tok.reshape(row_count * seq_len, model_dim)
    head_shape = (row_count, seq_len, H, HD)
    query = (plain_dot(tok_flat, w_query) + b_query).astype(jnp.bfloat16).reshape(head_shape)
    keys = plain_dot(tok_flat, w_key).astype(jnp.bfloat16).reshape(head_shape)
    values = (plain_dot(tok_flat, w_value) + b_value).astype(jnp.bfloat16).reshape(head_shape)
    context, log_total = lax.map(attend_row, (query, keys, values, seg_block))
    context = context.reshape(row_count * seq_len, model_dim)
    normed_attn, inv_attn = normalize(
        tok_flat.astype(jnp.float32) + plain_dot(context, w_out) + b_out
    )
    mid_state = normed_attn * gain_attn + shift_attn
    mid_low = mid_state.astype(jnp.bfloat16)
    inner = plain_dot(mid_low, w_inner) + b_inner
    cdf_value, slope = gelu_parts(inner)
    activ = (inner * cdf_value).astype(jnp.bfloat16)
    normed_ffn, inv_ffn = normalize(mid_state + plain_dot(activ, w_outer) + b_outer)
    final = normed_ffn * gain_ffn + shift_ffn
    saved = (
        query,
        keys,
        values,
        log_total,
        context,
        normed_attn,
        inv_attn,
        mid_low,
        inner,
        activ,
        normed_ffn,
        inv_ffn,
    )
    return (final, saved)


def backward_block(grad_final, block_tok, seg_block, weights, saved):
    (
        w_query,
        b_query,
        w_key,
        w_value,
        b_value,
        w_out,
        b_out,
        gain_attn,
        shift_attn,
        w_inner,
        b_inner,
        w_outer,
        b_outer,
        gain_ffn,
        shift_ffn,
    ) = weights
    (
        query,
        keys,
        values,
        log_total,
        context,
        normed_attn,
        inv_attn,
        mid_low,
        inner,
        activ,
        normed_ffn,
        inv_ffn,
    ) = saved
    row_count, seq_len, model_dim = block_tok.shape
    tok_flat = block_tok.reshape(row_count * seq_len, model_dim)
    grad_gain_ffn = jnp.sum(grad_final * normed_ffn, axis=0)
    grad_shift_ffn = jnp.sum(grad_final, axis=0)
    grad_h2 = norm_back(grad_final * gain_ffn, normed_ffn, inv_ffn)
    grad_branch = grad_h2.astype(jnp.bfloat16)
    grad_w_outer = cross_dot(activ, grad_branch)
    grad_b_outer = jnp.sum(grad_branch, axis=0, dtype=jnp.float32)
    cdf_value, slope = gelu_parts(inner)
    grad_inner = (back_dot(grad_branch, w_outer) * slope).astype(jnp.bfloat16)
    grad_w_inner = cross_dot(mid_low, grad_inner)
    grad_b_inner = jnp.sum(grad_inner, axis=0, dtype=jnp.float32)
    grad_mid = grad_h2 + back_dot(grad_inner, w_inner)
    grad_gain_attn = jnp.sum(grad_mid * normed_attn, axis=0)
    grad_shift_attn = jnp.sum(grad_mid, axis=0)
    grad_h1 = norm_back(grad_mid * gain_attn, normed_attn, inv_attn)
    grad_attn = grad_h1.astype(jnp.bfloat16)
    grad_w_out = cross_dot(context, grad_attn)
    grad_b_out = jnp.sum(grad_attn, axis=0, dtype=jnp.float32)
    grad_ctx = back_dot(grad_attn, w_out).astype(jnp.bfloat16).reshape(row_count, seq_len, H, HD)
    grad_query, grad_keys, grad_values = lax.map(
        attend_row_back, (query, keys, values, seg_block, log_total, grad_ctx)
    )
    flat_shape = (row_count * seq_len, model_dim)
    grad_query = grad_query.reshape(flat_shape)
    grad_keys = grad_keys.reshape(flat_shape)
    grad_values = grad_values.reshape(flat_shape)
    grad_w_query = cross_dot(tok_flat, grad_query)
    grad_b_query = jnp.sum(grad_query, axis=0, dtype=jnp.float32)
    grad_w_key = cross_dot(tok_flat, grad_keys)
    grad_w_value = cross_dot(tok_flat, grad_values)
    grad_b_value = jnp.sum(grad_values, axis=0, dtype=jnp.float32)
    grad_tok = (
        grad_h1
        + back_dot(grad_query, w_query)
        + back_dot(grad_keys, w_key)
        + back_dot(grad_values, w_value)
    )
    grads = (
        grad_w_query,
        grad_b_query,
        grad_w_key,
        grad_w_value,
        grad_b_value,
        grad_w_out,
        grad_b_out,
        grad_gain_attn,
        grad_shift_attn,
        grad_w_inner,
        grad_b_inner,
        grad_w_outer,
        grad_b_outer,
        grad_gain_ffn,
        grad_shift_ffn,
    )
    return (grad_tok.astype(jnp.bfloat16).reshape(row_count, seq_len, model_dim), grads)


def reduce_grads(grads):
    (
        grad_w_query,
        grad_b_query,
        grad_w_key,
        grad_w_value,
        grad_b_value,
        grad_w_out,
        grad_b_out,
        grad_gain_attn,
        grad_shift_attn,
        grad_w_inner,
        grad_b_inner,
        grad_w_outer,
        grad_b_outer,
        grad_gain_ffn,
        grad_shift_ffn,
    ) = grads
    (
        shard_w_query,
        shard_b_query,
        shard_w_key,
        shard_w_value,
        shard_b_value,
        shard_w_out,
        shard_b_out,
        shard_gain_attn,
        shard_shift_attn,
        shard_w_inner,
        shard_b_inner,
        shard_w_outer,
        shard_b_outer,
        shard_gain_ffn,
        shard_shift_ffn,
    ) = (
        lax.psum_scatter(
            grad_w_query.astype(jnp.bfloat16), "fsdp", scatter_dimension=0, tiled=True
        ).astype(jnp.float32),
        lax.psum_scatter(
            grad_b_query.astype(jnp.bfloat16), "fsdp", scatter_dimension=0, tiled=True
        ).astype(jnp.float32),
        lax.psum_scatter(
            grad_w_key.astype(jnp.bfloat16), "fsdp", scatter_dimension=0, tiled=True
        ).astype(jnp.float32),
        lax.psum_scatter(
            grad_w_value.astype(jnp.bfloat16), "fsdp", scatter_dimension=0, tiled=True
        ).astype(jnp.float32),
        lax.psum_scatter(
            grad_b_value.astype(jnp.bfloat16), "fsdp", scatter_dimension=0, tiled=True
        ).astype(jnp.float32),
        lax.psum_scatter(
            grad_w_out.astype(jnp.bfloat16), "fsdp", scatter_dimension=0, tiled=True
        ).astype(jnp.float32),
        lax.psum_scatter(
            grad_b_out.astype(jnp.bfloat16), "fsdp", scatter_dimension=0, tiled=True
        ).astype(jnp.float32),
        lax.psum_scatter(
            grad_gain_attn.astype(jnp.bfloat16), "fsdp", scatter_dimension=0, tiled=True
        ).astype(jnp.float32),
        lax.psum_scatter(
            grad_shift_attn.astype(jnp.bfloat16), "fsdp", scatter_dimension=0, tiled=True
        ).astype(jnp.float32),
        lax.psum_scatter(
            grad_w_inner.astype(jnp.bfloat16), "fsdp", scatter_dimension=0, tiled=True
        ).astype(jnp.float32),
        lax.psum_scatter(
            grad_b_inner.astype(jnp.bfloat16), "fsdp", scatter_dimension=0, tiled=True
        ).astype(jnp.float32),
        lax.psum_scatter(
            grad_w_outer.astype(jnp.bfloat16), "fsdp", scatter_dimension=0, tiled=True
        ).astype(jnp.float32),
        lax.psum_scatter(
            grad_b_outer.astype(jnp.bfloat16), "fsdp", scatter_dimension=0, tiled=True
        ).astype(jnp.float32),
        lax.psum_scatter(
            grad_gain_ffn.astype(jnp.bfloat16), "fsdp", scatter_dimension=0, tiled=True
        ).astype(jnp.float32),
        lax.psum_scatter(
            grad_shift_ffn.astype(jnp.bfloat16), "fsdp", scatter_dimension=0, tiled=True
        ).astype(jnp.float32),
    )
    return (
        lax.psum(shard_w_query.astype(jnp.bfloat16), ("twin", "dp")).astype(jnp.float32),
        lax.psum(shard_b_query.astype(jnp.bfloat16), ("twin", "dp")).astype(jnp.float32),
        lax.psum(shard_w_key.astype(jnp.bfloat16), ("twin", "dp")).astype(jnp.float32),
        lax.psum(shard_w_value.astype(jnp.bfloat16), ("twin", "dp")).astype(jnp.float32),
        lax.psum(shard_b_value.astype(jnp.bfloat16), ("twin", "dp")).astype(jnp.float32),
        lax.psum(shard_w_out.astype(jnp.bfloat16), ("twin", "dp")).astype(jnp.float32),
        lax.psum(shard_b_out.astype(jnp.bfloat16), ("twin", "dp")).astype(jnp.float32),
        lax.psum(shard_gain_attn.astype(jnp.bfloat16), ("twin", "dp")).astype(jnp.float32),
        lax.psum(shard_shift_attn.astype(jnp.bfloat16), ("twin", "dp")).astype(jnp.float32),
        lax.psum(shard_w_inner.astype(jnp.bfloat16), ("twin", "dp")).astype(jnp.float32),
        lax.psum(shard_b_inner.astype(jnp.bfloat16), ("twin", "dp")).astype(jnp.float32),
        lax.psum(shard_w_outer.astype(jnp.bfloat16), ("twin", "dp")).astype(jnp.float32),
        lax.psum(shard_b_outer.astype(jnp.bfloat16), ("twin", "dp")).astype(jnp.float32),
        lax.psum(shard_gain_ffn.astype(jnp.bfloat16), ("twin", "dp")).astype(jnp.float32),
        lax.psum(shard_shift_ffn.astype(jnp.bfloat16), ("twin", "dp")).astype(jnp.float32),
    )


def general_device(
    tokens,
    w_query,
    b_query,
    w_key,
    w_value,
    b_value,
    w_out,
    b_out,
    gain_attn,
    shift_attn,
    w_inner,
    b_inner,
    w_outer,
    b_outer,
    gain_ffn,
    shift_ffn,
    lengths,
    labels,
):
    row_total, seq_len, model_dim = tokens.shape
    block_rows = row_total // MB
    seg_all = segment_ids(lengths, seq_len)
    member = (seg_all[:, None, :] == jnp.arange(SEG, dtype=jnp.int32)[None, :, None]).astype(
        jnp.float32
    )
    counts = lengths[:, :SEG].astype(jnp.float32)
    finals = []
    saved_list = []
    for block_idx in range(MB):
        row_span = slice(block_idx * block_rows, (block_idx + 1) * block_rows)
        weights = (
            lax.all_gather(w_query, "fsdp", axis=0, tiled=True),
            lax.all_gather(b_query, "fsdp", axis=0, tiled=True),
            lax.all_gather(w_key, "fsdp", axis=0, tiled=True),
            lax.all_gather(w_value, "fsdp", axis=0, tiled=True),
            lax.all_gather(b_value, "fsdp", axis=0, tiled=True),
            lax.all_gather(w_out, "fsdp", axis=0, tiled=True),
            lax.all_gather(b_out, "fsdp", axis=0, tiled=True),
            lax.all_gather(gain_attn, "fsdp", axis=0, tiled=True),
            lax.all_gather(shift_attn, "fsdp", axis=0, tiled=True),
            lax.all_gather(w_inner, "fsdp", axis=0, tiled=True),
            lax.all_gather(b_inner, "fsdp", axis=0, tiled=True),
            lax.all_gather(w_outer, "fsdp", axis=0, tiled=True),
            lax.all_gather(b_outer, "fsdp", axis=0, tiled=True),
            lax.all_gather(gain_ffn, "fsdp", axis=0, tiled=True),
            lax.all_gather(shift_ffn, "fsdp", axis=0, tiled=True),
        )
        final, saved = forward_block(tokens[row_span], seg_all[row_span], weights)
        finals.append(final.reshape(block_rows, seq_len, model_dim))
        saved_list.append(saved)
    final_all = jnp.concatenate(finals, axis=0)
    pooled_f = (
        jnp.einsum("rst,rtd->rsd", member, final_all, precision=lax.Precision.HIGHEST)
        / counts[:, :, None]
    )
    pooled_low = pooled_f.reshape(row_total * SEG, model_dim).astype(jnp.bfloat16)
    gathered = lax.all_gather(pooled_low, ("twin", "dp", "fsdp"), axis=0, tiled=True)
    own_count = pooled_low.shape[0]
    half_count = labels.shape[0]
    twin_side = lax.axis_index("twin")
    device = lax.axis_index(("twin", "dp", "fsdp"))
    first_seg = device * own_count
    other_start = (1 - twin_side) * half_count
    other_side = lax.dynamic_slice_in_dim(gathered, other_start, half_count, 0)
    own_f = pooled_low.astype(jnp.float32)
    other_f = other_side.astype(jnp.float32)
    inv_own = lax.rsqrt(jnp.sum(own_f * own_f, axis=1) + pool_eps)
    inv_other = lax.rsqrt(jnp.sum(other_f * other_f, axis=1) + pool_eps)
    col_index = jnp.arange(half_count, dtype=jnp.int32)
    similar = sim_scale * back_dot(pooled_low, other_side) * inv_own[:, None] * inv_other[None, :]
    own_labels = lax.dynamic_slice_in_dim(
        labels, jnp.minimum(first_seg, half_count - own_count), own_count, 0
    )
    own_index = first_seg - half_count + jnp.arange(own_count, dtype=jnp.int32)
    target = jnp.where(
        twin_side == 0,
        col_index[None, :] == own_labels[:, None],
        labels[None, :] == own_index[:, None],
    ).astype(jnp.float32)
    row_max = jnp.max(similar, axis=1, keepdims=True)
    log_total = row_max[:, 0] + jnp.log(jnp.sum(jnp.exp(similar - row_max), axis=1))
    grad_sim = jnp.exp(similar - log_total[:, None]) - target
    weighted = grad_sim * similar
    grad_raw = sim_scale * grad_sim * inv_own[:, None] * inv_other[None, :]
    grad_own = (
        jnp.dot(grad_raw, other_f, precision=lax.Precision.HIGHEST)
        - (jnp.sum(weighted, axis=1) * inv_own * inv_own)[:, None] * own_f
    )
    grad_other = (
        lax.dot_general(grad_raw, own_f, (((0,), (0,)), ((), ())), precision=lax.Precision.HIGHEST)
        - (jnp.sum(weighted, axis=0) * inv_other * inv_other)[:, None] * other_f
    )
    term = jnp.zeros((2 * half_count, model_dim), jnp.float32)
    term = lax.dynamic_update_slice_in_dim(term, grad_other, other_start, 0)
    term = lax.dynamic_update_slice_in_dim(term, grad_own, first_seg, 0)
    grad_pooled = lax.psum_scatter(term, ("twin", "dp", "fsdp"), scatter_dimension=0, tiled=True)
    grad_scaled = grad_pooled.reshape(row_total, SEG, model_dim) / counts[:, :, None]
    grad_toks = []
    grad_total = None
    for block_idx in range(MB):
        row_span = slice(block_idx * block_rows, (block_idx + 1) * block_rows)
        weights = (
            lax.all_gather(w_query, "fsdp", axis=0, tiled=True),
            lax.all_gather(b_query, "fsdp", axis=0, tiled=True),
            lax.all_gather(w_key, "fsdp", axis=0, tiled=True),
            lax.all_gather(w_value, "fsdp", axis=0, tiled=True),
            lax.all_gather(b_value, "fsdp", axis=0, tiled=True),
            lax.all_gather(w_out, "fsdp", axis=0, tiled=True),
            lax.all_gather(b_out, "fsdp", axis=0, tiled=True),
            lax.all_gather(gain_attn, "fsdp", axis=0, tiled=True),
            lax.all_gather(shift_attn, "fsdp", axis=0, tiled=True),
            lax.all_gather(w_inner, "fsdp", axis=0, tiled=True),
            lax.all_gather(b_inner, "fsdp", axis=0, tiled=True),
            lax.all_gather(w_outer, "fsdp", axis=0, tiled=True),
            lax.all_gather(b_outer, "fsdp", axis=0, tiled=True),
            lax.all_gather(gain_ffn, "fsdp", axis=0, tiled=True),
            lax.all_gather(shift_ffn, "fsdp", axis=0, tiled=True),
        )
        grad_final = jnp.einsum(
            "rst,rsd->rtd", member[row_span], grad_scaled[row_span], precision=lax.Precision.HIGHEST
        ).reshape(block_rows * seq_len, model_dim)
        grad_tok, grads = backward_block(
            grad_final, tokens[row_span], seg_all[row_span], weights, saved_list[block_idx]
        )
        grad_toks.append(grad_tok)
        grads = reduce_grads(grads)
        grad_total = grads if grad_total is None else jax.tree.map(jnp.add, grad_total, grads)
    output = final_all.astype(jnp.bfloat16)
    grad_tokens = jnp.concatenate(grad_toks, axis=0)
    return (output, grad_tokens) + tuple(grad_total)


def solution(mesh):
    placed = (
        P(("twin", "dp", "fsdp"), None, None),
        P("fsdp", None),
        P("fsdp"),
        P("fsdp", None),
        P("fsdp", None),
        P("fsdp"),
        P("fsdp", None),
        P("fsdp"),
        P("fsdp"),
        P("fsdp"),
        P("fsdp", None),
        P("fsdp"),
        P("fsdp", None),
        P("fsdp"),
        P("fsdp"),
        P("fsdp"),
        P(("twin", "dp", "fsdp"), None),
        P(),
    )
    sizes = (mesh.shape["twin"], mesh.shape["dp"], mesh.shape["fsdp"])
    return jax.shard_map(
        per_device if sizes == (2, 4, 4) else general_device,
        mesh=mesh,
        in_specs=placed,
        out_specs=(
            P(("twin", "dp", "fsdp"), None, None),
            P(("twin", "dp", "fsdp"), None, None),
            P("fsdp", None),
            P("fsdp"),
            P("fsdp", None),
            P("fsdp", None),
            P("fsdp"),
            P("fsdp", None),
            P("fsdp"),
            P("fsdp"),
            P("fsdp"),
            P("fsdp", None),
            P("fsdp"),
            P("fsdp", None),
            P("fsdp"),
            P("fsdp"),
            P("fsdp"),
        ),
        check_vma=False,
    )
```

```python
import jax
import jax.numpy as jnp
from jax import lax
from jax.experimental import pallas as pl
from jax.experimental.pallas import tpu as pltpu
from jax.sharding import PartitionSpec as P

H = 12
HD = 64
SEG = 8
MB = 2
TQ = 128


norm_eps = 1e-12
pool_eps = 1e-06
sim_scale = 20.0


def cross_dot(left, right):
    return lax.dot_general(
        left, right, (((0,), (0,)), ((), ())), preferred_element_type=jnp.float32
    )


def back_dot(left, right):
    return lax.dot_general(
        left, right, (((1,), (1,)), ((), ())), preferred_element_type=jnp.float32
    )


def plain_dot(left, right):
    return jnp.dot(left, right, preferred_element_type=jnp.float32)


def segment_ids(lengths, seq_len):
    ends = jnp.cumsum(lengths, axis=1, dtype=jnp.int32)
    position = jnp.arange(seq_len, dtype=jnp.int32)
    return jnp.sum((position[None, :, None] >= ends[:, None, :]).astype(jnp.int32), axis=2)


def normalize(hidden):
    centred = hidden - jnp.mean(hidden, axis=-1, keepdims=True)
    inv_dev = lax.rsqrt(jnp.mean(centred * centred, axis=-1, keepdims=True) + norm_eps)
    return (centred * inv_dev, inv_dev)


def norm_back(grad_normed, normed, inv_dev):
    return inv_dev * (
        grad_normed
        - jnp.mean(grad_normed, axis=-1, keepdims=True)
        - normed * jnp.mean(grad_normed * normed, axis=-1, keepdims=True)
    )


def gelu_parts(inner):
    cdf_value = 0.5 * (1.0 + lax.erf(inner * 0.7071067811865476))
    slope = cdf_value + inner * jnp.exp(-0.5 * inner * inner) * 0.3989422804014327
    return (cdf_value, slope)


def key_span(tile, seq_len):
    return max(0, (tile - 1) * TQ), min(seq_len, (tile + 2) * TQ)


def split_heads(block):
    lane = lax.broadcasted_iota(jnp.int32, block.shape, 1)
    zero = jnp.zeros_like(block)
    return jnp.concatenate(
        [jnp.where(lane < HD, block, zero), jnp.where(lane < HD, zero, block)], axis=0
    )


def merge_heads(double):
    count = double.shape[0] // 2
    lane = lax.broadcasted_iota(jnp.int32, (count, double.shape[1]), 1)
    return jnp.where(lane < HD, double[:count], double[count:])


def fill_bias(seg_col_ref, seg_row_ref, bias_ref, seq_len):
    for tile in range(seq_len // TQ):
        low, high = key_span(tile, seq_len)
        same = seg_col_ref[low:high, :] == seg_row_ref[:, tile * TQ : (tile + 1) * TQ]
        bias_ref[tile, : high - low, :] = jnp.where(same, 0.0, -1e30)


def attend_kernel(seg_col_ref, seg_row_ref, tok_ref, qkv_ref, ctx_ref, log_ref, bias_ref):
    seq_len = tok_ref.shape[0]

    @pl.when(pl.program_id(1) == 0)
    def _():
        fill_bias(seg_col_ref, seg_row_ref, bias_ref, seq_len)

    ctx_ref[0] = tok_ref[...]
    for tile in range(seq_len // TQ):
        low, high = key_span(tile, seq_len)
        rows = slice(tile * TQ, (tile + 1) * TQ)
        query = split_heads(qkv_ref[0, rows, :] * jnp.bfloat16(HD**-0.5))
        bias = bias_ref[tile, : high - low, :]
        scores = back_dot(qkv_ref[1, low:high, :], query) + jnp.concatenate([bias, bias], axis=1)
        top = jnp.max(scores, axis=0, keepdims=True)
        exp_scores = jnp.exp(scores - top)
        row_sum = jnp.sum(exp_scores, axis=0, keepdims=True)
        prob = (exp_scores * (1.0 / row_sum)).astype(jnp.bfloat16)
        context = cross_dot(prob, qkv_ref[2, low:high, :])
        ctx_ref[1, rows, :] = merge_heads(context).astype(jnp.bfloat16)
        log_ref[0, 0, tile : tile + 1, :] = top + jnp.log(row_sum)


def attend_back_kernel(
    seg_col_ref, seg_row_ref, qkv_ref, grad_ref, log_ref, attn_ref, out_ref, bias_ref, key_acc, val_acc
):
    seq_len = attn_ref.shape[0]

    @pl.when(pl.program_id(1) == 0)
    def _():
        fill_bias(seg_col_ref, seg_row_ref, bias_ref, seq_len)

    key_acc[...] = jnp.zeros_like(key_acc)
    val_acc[...] = jnp.zeros_like(val_acc)
    out_ref[3] = attn_ref[...]
    for tile in range(seq_len // TQ):
        low, high = key_span(tile, seq_len)
        rows = slice(tile * TQ, (tile + 1) * TQ)
        query = split_heads(qkv_ref[0, rows, :] * jnp.bfloat16(HD**-0.5))
        grad = split_heads(grad_ref[rows, :])
        bias = bias_ref[tile, : high - low, :]
        keys = qkv_ref[1, low:high, :]
        scores = back_dot(keys, query) + jnp.concatenate([bias, bias], axis=1)
        prob = jnp.exp(scores - log_ref[0, 0, tile : tile + 1, :])
        grad_prob = back_dot(qkv_ref[2, low:high, :], grad)
        total = jnp.sum(prob * grad_prob, axis=0, keepdims=True)
        grad_scores = (prob * (grad_prob - total)).astype(jnp.bfloat16)
        val_acc[low:high, :] += plain_dot(prob.astype(jnp.bfloat16), grad)
        key_acc[low:high, :] += plain_dot(grad_scores, query)
        grad_query = merge_heads(cross_dot(grad_scores, keys))
        out_ref[0, rows, :] = (grad_query * HD**-0.5).astype(jnp.bfloat16)
    out_ref[1] = key_acc[...].astype(jnp.bfloat16)
    out_ref[2] = val_acc[...].astype(jnp.bfloat16)


def attend(seg_all, tok_flat, qkv):
    row_count, seq_len = seg_all.shape
    token_count, model_dim = tok_flat.shape
    pairs = model_dim // (2 * HD)
    tiles = seq_len // TQ
    return pl.pallas_call(
        attend_kernel,
        grid=(row_count, pairs),
        in_specs=[
            pl.BlockSpec((None, seq_len, 1), lambda r, p: (r, 0, 0)),
            pl.BlockSpec((None, 1, seq_len), lambda r, p: (r, 0, 0)),
            pl.BlockSpec((seq_len, 2 * HD), lambda r, p: (r, p)),
            pl.BlockSpec((3, seq_len, 2 * HD), lambda r, p: (0, r, p)),
        ],
        out_specs=[
            pl.BlockSpec((2, seq_len, 2 * HD), lambda r, p: (0, r, p)),
            pl.BlockSpec((1, 1, tiles, 2 * TQ), lambda r, p: (r, p, 0, 0)),
        ],
        out_shape=[
            jax.ShapeDtypeStruct((2, token_count, model_dim), jnp.bfloat16),
            jax.ShapeDtypeStruct((row_count, pairs, tiles, 2 * TQ), jnp.float32),
        ],
        scratch_shapes=[pltpu.VMEM((tiles, 3 * TQ, TQ), jnp.float32)],
        cost_estimate=pl.CostEstimate(
            flops=4 * token_count * 3 * TQ * model_dim * 2,
            bytes_accessed=token_count * model_dim * 14,
            transcendentals=token_count * 3 * TQ * 2 * pairs,
        ),
        name="attend",
    )(seg_all[:, :, None], seg_all[:, None, :], tok_flat, qkv)


def attend_back(seg_all, qkv, grad_ctx, log_total, grad_attn):
    row_count, seq_len = seg_all.shape
    token_count, model_dim = grad_ctx.shape
    pairs = model_dim // (2 * HD)
    tiles = seq_len // TQ
    flat = pl.BlockSpec((seq_len, 2 * HD), lambda r, p: (r, p))
    return pl.pallas_call(
        attend_back_kernel,
        grid=(row_count, pairs),
        in_specs=[
            pl.BlockSpec((None, seq_len, 1), lambda r, p: (r, 0, 0)),
            pl.BlockSpec((None, 1, seq_len), lambda r, p: (r, 0, 0)),
            pl.BlockSpec((3, seq_len, 2 * HD), lambda r, p: (0, r, p)),
            flat,
            pl.BlockSpec((1, 1, tiles, 2 * TQ), lambda r, p: (r, p, 0, 0)),
            flat,
        ],
        out_specs=pl.BlockSpec((4, seq_len, 2 * HD), lambda r, p: (0, r, p)),
        out_shape=jax.ShapeDtypeStruct((4, token_count, model_dim), jnp.bfloat16),
        scratch_shapes=[
            pltpu.VMEM((tiles, 3 * TQ, TQ), jnp.float32),
            pltpu.VMEM((seq_len, 2 * HD), jnp.float32),
            pltpu.VMEM((seq_len, 2 * HD), jnp.float32),
        ],
        cost_estimate=pl.CostEstimate(
            flops=10 * token_count * 3 * TQ * model_dim * 2,
            bytes_accessed=token_count * model_dim * 20,
            transcendentals=token_count * 3 * TQ * 2 * pairs,
        ),
        name="attend_back",
    )(seg_all[:, :, None], seg_all[:, None, :], qkv, grad_ctx, log_total, grad_attn)


def swap(value, axis_name, bit):
    count = 2 if axis_name == "twin" else 4
    return lax.ppermute(value, axis_name, [(i, i ^ bit) for i in range(count)])


def hold(values):
    return lax.optimization_barrier(values)


def across_depth(piece):
    return jnp.stack([swap(piece, "fsdp", s) for s in (1, 2, 3)])


def assemble_wide_kernel(place_ref, *refs):
    step = pl.program_id(0)
    out_ref = refs[-1]
    count = len(refs) - 3
    near_ref, far_ref = refs[count], refs[count + 1]
    model_dim = near_ref.shape[-1]
    half = near_ref.shape[-2]

    @pl.when(step == 0)
    def _():
        if count == 1:
            out_ref[...] = refs[0][...]
        else:
            for index in range(count):
                out_ref[:, index * model_dim : (index + 1) * model_dim] = refs[index][...]

    @pl.when(step > 0)
    def _():
        for index in range(8):
            spot = place_ref[1] ^ index
            source = near_ref if index < 4 else far_ref
            row = pl.multiple_of((spot % 2) * half, half)
            column = pl.multiple_of((spot // 2) * model_dim, model_dim)
            out_ref[pl.ds(row, half), pl.ds(column, model_dim)] = source[index % 4]


def assemble_tall_kernel(place_ref, shard_ref, near_ref, far_ref, out_ref):
    step = pl.program_id(0)
    half = near_ref.shape[-2]

    @pl.when(step == 0)
    def _():
        out_ref[...] = shard_ref[...]

    @pl.when(step > 0)
    def _():
        for index in range(8):
            source = near_ref if index < 4 else far_ref
            row = pl.multiple_of((place_ref[1] ^ index) * half, half)
            out_ref[pl.ds(row, half), :] = source[index % 4]


def assemble(kernel, place, shards, near, far, part, name):
    rows = shards[0].shape[0]
    columns = sum(shard.shape[1] for shard in shards)
    half, model_dim = near.shape[-2:]
    gathered = pl.BlockSpec(
        (4, None, None, half, model_dim),
        lambda s, place: (0, jnp.maximum(s - 1, 0), part, 0, 0),
    )
    return pl.pallas_call(
        kernel,
        grid_spec=pltpu.PrefetchScalarGridSpec(
            num_scalar_prefetch=1,
            grid=(4,),
            in_specs=[pl.BlockSpec(shard.shape, lambda s, place: (0, 0)) for shard in shards]
            + [gathered, gathered],
            out_specs=pl.BlockSpec((rows, columns), lambda s, place: (place[0] ^ s, 0)),
        ),
        out_shape=jax.ShapeDtypeStruct((4 * rows, columns), jnp.bfloat16),
        cost_estimate=pl.CostEstimate(
            flops=0, bytes_accessed=16 * rows * columns, transcendentals=0
        ),
        name=name,
    )(place, *shards, near, far)


def project_kernel(tok_ref, weight_ref, bias_ref, out_ref):
    out_ref[...] = (plain_dot(tok_ref[...], weight_ref[...]) + bias_ref[0]).astype(jnp.bfloat16)


def project(tok_flat, square, biases):
    token_count, model_dim = tok_flat.shape
    return pl.pallas_call(
        project_kernel,
        grid=(3,),
        in_specs=[
            pl.BlockSpec((token_count, model_dim), lambda m: (0, 0)),
            pl.BlockSpec((model_dim, model_dim), lambda m: (0, m)),
            pl.BlockSpec((1, 1, model_dim), lambda m: (m, 0, 0)),
        ],
        out_specs=pl.BlockSpec((None, token_count, model_dim), lambda m: (m, 0, 0)),
        out_shape=jax.ShapeDtypeStruct((3, token_count, model_dim), jnp.bfloat16),
        cost_estimate=pl.CostEstimate(
            flops=6 * token_count * model_dim**2,
            bytes_accessed=8 * token_count * model_dim,
            transcendentals=0,
        ),
        name="project",
    )(tok_flat, square, biases)


def project_back_kernel(grad_ref, weight_ref, base_ref, out_ref, acc_ref):
    step = pl.program_id(0)

    @pl.when(step == 0)
    def _():
        acc_ref[...] = base_ref[...]

    acc_ref[...] += back_dot(grad_ref[...], weight_ref[...])

    @pl.when(step == 2)
    def _():
        out_ref[...] = acc_ref[...].astype(jnp.bfloat16)


def project_back(grads, square, base):
    _, token_count, model_dim = grads.shape
    return pl.pallas_call(
        project_back_kernel,
        grid=(3,),
        in_specs=[
            pl.BlockSpec((None, token_count, model_dim), lambda m: (m, 0, 0)),
            pl.BlockSpec((model_dim, model_dim), lambda m: (0, m)),
            pl.BlockSpec((token_count, model_dim), lambda m: (0, 0)),
        ],
        out_specs=pl.BlockSpec((token_count, model_dim), lambda m: (0, 0)),
        out_shape=jax.ShapeDtypeStruct((token_count, model_dim), jnp.bfloat16),
        scratch_shapes=[pltpu.VMEM((token_count, model_dim), jnp.float32)],
        cost_estimate=pl.CostEstimate(
            flops=6 * token_count * model_dim**2,
            bytes_accessed=8 * token_count * model_dim,
            transcendentals=0,
        ),
        name="project_back",
    )(grads, square, base)


def weight_grad_kernel(place_ref, left_ref, right_ref, out_ref, acc_ref):
    acc_ref[...] = cross_dot(left_ref[...], right_ref[...])
    half = out_ref.shape[-2]
    for x in range(2):
        for z in range(4):
            row = pl.multiple_of(
                ((place_ref[0] ^ z) * 2 + ((place_ref[1] ^ x) % 2)) * half, half
            )
            out_ref[x, z] = acc_ref[pl.ds(row, half), :].astype(jnp.bfloat16)


def weight_grad_tall_kernel(place_ref, left_ref, right_ref, out_ref, acc_ref):
    acc_ref[...] = cross_dot(left_ref[...], right_ref[...])
    half = out_ref.shape[-2]
    for index in range(4):
        row = pl.multiple_of(((place_ref[1] ^ index) % 4) * half, half)
        out_ref[index // 2, index % 2] = acc_ref[pl.ds(row, half), :].astype(jnp.bfloat16)


def weight_grad(kind, side, place, left, right):
    token_count = left.shape[-2]
    model_dim = left.shape[-1] if kind != "tall" else right.shape[-1]
    half = model_dim // 8
    block = lambda y, place: (place[1] // 2) ^ (2 * side + y)
    if kind == "square":
        left_spec = pl.BlockSpec(
            (None, token_count, model_dim), lambda y, place: (block(y, place) // 3, 0, 0)
        )
        right_spec = pl.BlockSpec(
            (None, token_count, model_dim), lambda y, place: (block(y, place), 0, 0)
        )
    elif kind == "wide":
        left_spec = pl.BlockSpec((token_count, model_dim), lambda y, place: (0, 0))
        right_spec = pl.BlockSpec((token_count, model_dim), lambda y, place: (0, block(y, place)))
    if kind == "tall":
        return pl.pallas_call(
            weight_grad_tall_kernel,
            grid_spec=pltpu.PrefetchScalarGridSpec(
                num_scalar_prefetch=1,
                grid=(4,),
                in_specs=[
                    pl.BlockSpec(
                        (token_count, model_dim // 2),
                        lambda z, place: (0, (place[0] ^ z) * 2 + ((place[1] // 4) ^ side)),
                    ),
                    pl.BlockSpec((token_count, model_dim), lambda z, place: (0, 0)),
                ],
                out_specs=pl.BlockSpec(
                    (2, 2, None, half, model_dim), lambda z, place: (0, 0, z, 0, 0)
                ),
                scratch_shapes=[pltpu.VMEM((model_dim // 2, model_dim), jnp.float32)],
            ),
            out_shape=jax.ShapeDtypeStruct((2, 2, 4, half, model_dim), jnp.bfloat16),
            cost_estimate=pl.CostEstimate(
                flops=4 * token_count * model_dim**2,
                bytes_accessed=8 * token_count * model_dim,
                transcendentals=0,
            ),
            name="weight_grad_tall",
        )(place, left, right)
    return pl.pallas_call(
        weight_grad_kernel,
        grid_spec=pltpu.PrefetchScalarGridSpec(
            num_scalar_prefetch=1,
            grid=(2,),
            in_specs=[left_spec, right_spec],
            out_specs=pl.BlockSpec(
                (None, 2, 4, half, model_dim), lambda y, place: (y, 0, 0, 0, 0)
            ),
            scratch_shapes=[pltpu.VMEM((model_dim, model_dim), jnp.float32)],
        ),
        out_shape=jax.ShapeDtypeStruct((2, 2, 4, half, model_dim), jnp.bfloat16),
        cost_estimate=pl.CostEstimate(
            flops=4 * token_count * model_dim**2,
            bytes_accessed=8 * token_count * model_dim,
            transcendentals=0,
        ),
        name="weight_grad_" + kind,
    )(place, left, right)


def add_low(*parts):
    total = parts[0].astype(jnp.float32)
    for part in parts[1:]:
        total = total + part.astype(jnp.float32)
    return total.astype(jnp.bfloat16)


def gather_back(piece):
    pair = jnp.stack([piece, swap(piece, "dp", 1)])
    quad = jnp.concatenate([pair, swap(pair, "dp", 2)])
    return quad, swap(quad, "twin", 1)


def scatter_out_kernel(place_ref, quad_a, far_a, quad_b, far_b, *outs):
    half, model_dim = quad_a.shape[-2:]
    for index in range(8):
        spot = place_ref[1] ^ index
        pick = lambda near, far: (near if index < 4 else far)[index % 4]
        value = pick(quad_a, far_a).astype(jnp.float32)
        row = pl.multiple_of((spot % 2) * half, half)
        for matrix in range(4):

            @pl.when(spot // 2 == matrix)
            def _():
                outs[matrix][pl.ds(row, half), :] = value

        column = pl.multiple_of((spot // 2) * model_dim, model_dim)
        both = pick(quad_b, far_b)
        outs[4][pl.ds(row, half), pl.ds(column, model_dim)] = both[1].astype(jnp.float32)
        tall_row = pl.multiple_of(spot * half, half)
        outs[5][pl.ds(tall_row, half), :] = both[0].astype(jnp.float32)


def scatter_out(place, gathered_a, gathered_b):
    half, model_dim = gathered_a[0].shape[-2:]
    shard = 2 * half
    whole = pl.BlockSpec(memory_space=pltpu.VMEM)
    shapes = [(shard, model_dim)] * 4 + [(shard, 4 * model_dim), (4 * shard, model_dim)]
    return pl.pallas_call(
        scatter_out_kernel,
        in_specs=[pl.BlockSpec(memory_space=pltpu.SMEM)] + [whole] * 4,
        out_specs=[whole] * 6,
        out_shape=[jax.ShapeDtypeStruct(shape, jnp.float32) for shape in shapes],
        name="scatter_out",
    )(place, *gathered_a, *gathered_b)


def loss_grad(pooled_low, labels):
    own_count, model_dim = pooled_low.shape
    half_count = labels.shape[0]
    same = jnp.stack([pooled_low, swap(pooled_low, "dp", 1)])
    same = jnp.concatenate([same, swap(same, "dp", 2)])
    same = jnp.stack([same] + [swap(same, "fsdp", s) for s in (1, 2, 3)])
    same = same.reshape(half_count, model_dim)
    other = swap(same, "twin", 1)
    twin_side = lax.axis_index("twin")
    group, depth = lax.axis_index("dp"), lax.axis_index("fsdp")
    first = (group * 4 + depth) * own_count
    offset = jnp.arange(4, dtype=jnp.int32)
    numbers = ((offset[None, :] ^ group) * 4 + (offset[:, None] ^ depth)).reshape(16)
    numbers = (
        numbers[:, None] * own_count + jnp.arange(own_count, dtype=jnp.int32)[None, :]
    ).reshape(half_count)
    own_f = pooled_low.astype(jnp.float32)
    same_f = same.astype(jnp.float32)
    other_f = other.astype(jnp.float32)
    inv_own = lax.rsqrt(jnp.sum(own_f * own_f, axis=1) + pool_eps)
    inv_same = lax.rsqrt(jnp.sum(same_f * same_f, axis=1) + pool_eps)
    inv_other = lax.rsqrt(jnp.sum(other_f * other_f, axis=1) + pool_eps)
    similar = sim_scale * back_dot(same, other) * inv_same[:, None] * inv_other[None, :]
    col_max = jnp.max(similar, axis=0, keepdims=True)
    col_log = col_max[0] + jnp.log(jnp.sum(jnp.exp(similar - col_max), axis=0))
    own_sim = similar[:own_count]
    row_max = jnp.max(own_sim, axis=1, keepdims=True)
    row_log = row_max[:, 0] + jnp.log(jnp.sum(jnp.exp(own_sim - row_max), axis=1))
    own_labels = lax.dynamic_slice_in_dim(labels, first, own_count, 0)
    own_index = first + jnp.arange(own_count, dtype=jnp.int32)
    other_labels = labels[numbers]
    target = jnp.where(
        twin_side == 0,
        numbers[None, :] == own_labels[:, None],
        other_labels[None, :] == own_index[:, None],
    ).astype(jnp.float32)
    grad_sim = (
        jnp.exp(own_sim - row_log[:, None]) + jnp.exp(own_sim - col_log[None, :]) - 2.0 * target
    )
    grad_raw = sim_scale * grad_sim * inv_own[:, None] * inv_other[None, :]
    return (
        jnp.dot(grad_raw, other_f, precision=lax.Precision.HIGHEST)
        - (jnp.sum(grad_sim * own_sim, axis=1) * inv_own * inv_own)[:, None] * own_f
    )


def per_device(
    tokens,
    w_query,
    b_query,
    w_key,
    w_value,
    b_value,
    w_out,
    b_out,
    gain_attn,
    shift_attn,
    w_inner,
    b_inner,
    w_outer,
    b_outer,
    gain_ffn,
    shift_ffn,
    lengths,
    labels,
):
    row_total, seq_len, model_dim = tokens.shape
    token_count = row_total * seq_len
    shard = w_query.shape[0]
    half = shard // 2
    inner_dim = w_inner.shape[1]
    eighth = lax.axis_index("twin") * 4 + lax.axis_index("dp")
    depth = lax.axis_index("fsdp")
    place = jnp.stack([depth, eighth]).astype(jnp.int32)
    tok_flat = tokens.reshape(token_count, model_dim)

    stacked = jnp.stack([w_query, w_key, w_value, w_out]).reshape(8, half, model_dim)
    piece_a = lax.dynamic_index_in_dim(stacked, eighth, 0)
    piece_b = lax.dynamic_slice(
        w_inner, ((eighth % 2) * half, (eighth // 2) * model_dim), (half, model_dim)
    )
    piece_c = lax.dynamic_slice_in_dim(w_outer, eighth * half, half, 0)
    vectors = jnp.stack(
        [b_query, b_value, b_out, gain_attn, shift_attn, b_outer, gain_ffn, shift_ffn]
    )
    vectors = jnp.concatenate([vectors.reshape(8 * shard), b_inner])
    around = [vectors] + [swap(vectors, "fsdp", s) for s in (1, 2, 3)]
    ordered = jnp.stack(
        [sum(jnp.where(depth == z ^ s, around[s], 0) for s in range(4)) for z in range(4)]
    ).astype(jnp.float32)
    small = ordered[:, : 8 * shard].reshape(4, 8, shard).swapaxes(0, 1).reshape(8, model_dim)
    full_b_inner = ordered[:, 8 * shard :].reshape(inner_dim)
    seg_all = segment_ids(lengths, seq_len)
    member = (seg_all[:, None, :] == jnp.arange(SEG, dtype=jnp.int32)[None, :, None]).astype(
        jnp.float32
    )
    counts = lengths[:, :SEG].astype(jnp.float32)
    own_a = across_depth(piece_a)
    own_a, piece_bc, small, full_b_inner, seg_all, member = hold(
        (own_a, jnp.stack([piece_b, piece_c]), small, full_b_inner, seg_all, member)
    )
    beside_a, above_a = swap(own_a, "dp", 1), swap(own_a, "dp", 2)
    own_b = across_depth(piece_bc)
    beside_a, above_a, own_b = hold((beside_a, above_a, own_b))
    near_a = jnp.stack([own_a, beside_a, above_a, swap(beside_a, "dp", 2)])
    beside_b, above_b = swap(own_b, "dp", 1), swap(own_b, "dp", 2)
    far_a = swap(near_a, "twin", 1)
    b_query, b_value, b_out, gain_attn, shift_attn, b_outer, gain_ffn, shift_ffn = small
    biases = jnp.stack([b_query, jnp.zeros_like(b_query), b_value])[:, None]
    square = assemble(
        assemble_wide_kernel, place, [w_query, w_key, w_value, w_out], near_a, far_a, 0, "assemble_a"
    )
    square, beside_b, above_b = hold((square, beside_b, above_b))
    full_w_out = square[:, 3 * model_dim :]
    corner_b = jnp.concatenate(
        [swap(beside_b[:, :1], "dp", 2), swap(above_b[:, 1:], "dp", 1)], axis=1
    )
    qkv = project(tok_flat, square, biases)
    qkv, corner_b = hold((qkv, corner_b))
    near_b = jnp.stack([own_b, beside_b, above_b, corner_b])
    far_b = swap(near_b, "twin", 1)
    tok_ctx, log_total = attend(seg_all, tok_flat, qkv)
    tok_ctx, log_total, near_b, far_b = hold((tok_ctx, log_total, near_b, far_b))
    wide = assemble(assemble_wide_kernel, place, [w_inner], near_b, far_b, 0, "assemble_b")
    tall = assemble(assemble_tall_kernel, place, [w_outer], near_b, far_b, 1, "assemble_c")
    context = tok_ctx[1]
    normed_attn, inv_attn = normalize(
        tok_flat.astype(jnp.float32) + plain_dot(context, full_w_out) + b_out
    )
    mid_state = normed_attn * gain_attn + shift_attn
    mid_low = mid_state.astype(jnp.bfloat16)
    inner = plain_dot(mid_low, wide) + full_b_inner
    cdf_value, slope = gelu_parts(inner)
    activ = (inner * cdf_value).astype(jnp.bfloat16)
    normed_ffn, inv_ffn = normalize(mid_state + plain_dot(activ, tall) + b_outer)
    final = normed_ffn * gain_ffn + shift_ffn
    output = final.astype(jnp.bfloat16).reshape(row_total, seq_len, model_dim)
    pooled_f = (
        jnp.einsum(
            "rst,rtd->rsd",
            member,
            final.reshape(row_total, seq_len, model_dim),
            precision=lax.Precision.HIGHEST,
        )
        / counts[:, :, None]
    )
    pooled_low = pooled_f.reshape(row_total * SEG, model_dim).astype(jnp.bfloat16)
    grad_pooled = loss_grad(pooled_low, labels)
    grad_scaled = grad_pooled.reshape(row_total, SEG, model_dim) / counts[:, :, None]
    grad_final = jnp.einsum(
        "rst,rsd->rtd", member, grad_scaled, precision=lax.Precision.HIGHEST
    ).reshape(token_count, model_dim)

    grad_gain_ffn = jnp.sum(grad_final * normed_ffn, axis=0)
    grad_shift_ffn = jnp.sum(grad_final, axis=0)
    grad_h2 = norm_back(grad_final * gain_ffn, normed_ffn, inv_ffn)
    grad_branch = grad_h2.astype(jnp.bfloat16)
    sent_c = swap(weight_grad("tall", 1, place, activ, grad_branch), "twin", 1)
    mine_c = weight_grad("tall", 0, place, activ, grad_branch)
    grad_b_outer = jnp.sum(grad_branch, axis=0, dtype=jnp.float32)
    mine_c, grad_branch = hold((mine_c, grad_branch))
    grad_inner = (back_dot(grad_branch, tall) * slope).astype(jnp.bfloat16)
    sent_c, grad_inner = hold((sent_c, grad_inner))
    other_c = swap(add_low(mine_c[:, 1], sent_c[:, 1]), "dp", 1)
    sent_b = swap(weight_grad("wide", 1, place, mid_low, grad_inner), "twin", 1)
    mine_b = weight_grad("wide", 0, place, mid_low, grad_inner)
    mine_b, grad_inner = hold((mine_b, grad_inner))
    grad_b_inner = jnp.sum(grad_inner, axis=0, dtype=jnp.float32)
    grad_mid = grad_h2 + back_dot(grad_inner, wide)
    other_c, sent_b, grad_mid = hold((other_c, sent_b, grad_mid))
    last_c = swap(add_low(mine_c[1, 0], sent_c[1, 0], other_c[1]), "dp", 2)
    other_b = swap(add_low(mine_b[1], sent_b[1]), "dp", 2)
    grad_gain_attn = jnp.sum(grad_mid * normed_attn, axis=0)
    grad_shift_attn = jnp.sum(grad_mid, axis=0)
    grad_h1 = norm_back(grad_mid * gain_attn, normed_attn, inv_attn)
    grad_attn = grad_h1.astype(jnp.bfloat16)
    grad_b_out = jnp.sum(grad_attn, axis=0, dtype=jnp.float32)
    grad_ctx = back_dot(grad_attn, full_w_out).astype(jnp.bfloat16)
    grads = attend_back(seg_all, qkv, grad_ctx, log_total, grad_attn)
    last_c, other_b, grads = hold((last_c, other_b, grads))
    done_c = add_low(mine_c[0, 0], sent_c[0, 0], other_c[0], last_c)
    last_b = swap(add_low(mine_b[0, 1], sent_b[0, 1], other_b[1]), "dp", 1)
    parts_c = [swap(done_c[s], "fsdp", s) for s in (1, 2, 3)]
    sent_a = swap(weight_grad("square", 1, place, tok_ctx, grads), "twin", 1)
    mine_a = weight_grad("square", 0, place, tok_ctx, grads)
    last_b, parts_c, sent_a, mine_a, grads = hold((last_b, parts_c, sent_a, mine_a, grads))
    done_b = add_low(mine_b[0, 0], sent_b[0, 0], other_b[0], last_b)
    other_y = swap(add_low(mine_a[1, :, :2], sent_a[1, :, :2]), "dp", 2)
    other_x = swap(add_low(mine_a[:, 1, 2:], sent_a[:, 1, 2:]), "dp", 1)
    parts_b = [swap(done_b[s], "fsdp", s) for s in (1, 2, 3)]
    grad_b_query = jnp.sum(grads[0], axis=0, dtype=jnp.float32)
    grad_b_value = jnp.sum(grads[2], axis=0, dtype=jnp.float32)
    grad_tokens = project_back(grads, square, grad_h1)
    other_y, other_x, parts_b, grad_tokens = hold((other_y, other_x, parts_b, grad_tokens))
    grad_tokens = grad_tokens.reshape(row_total, seq_len, model_dim)
    last_y = swap(add_low(mine_a[0, 1, :2], sent_a[0, 1, :2], other_y[1]), "dp", 1)
    last_x = swap(add_low(mine_a[1, 0, 2:], sent_a[1, 0, 2:], other_x[1]), "dp", 2)
    back_cb = gather_back(
        jnp.stack([add_low(done_c[0], *parts_c), add_low(done_b[0], *parts_b)])
    )
    done_y = add_low(mine_a[0, 0, :2], sent_a[0, 0, :2], other_y[0], last_y)
    done_x = add_low(mine_a[0, 0, 2:], sent_a[0, 0, 2:], other_x[0], last_x)
    back_a = gather_back(
        add_low(
            done_y[0],
            swap(done_y[1], "fsdp", 1),
            swap(done_x[0], "fsdp", 2),
            swap(done_x[1], "fsdp", 3),
        )
    )

    vec = jnp.stack(
        [
            grad_b_query,
            grad_b_value,
            grad_b_out,
            grad_gain_attn,
            grad_shift_attn,
            grad_b_outer,
            grad_gain_ffn,
            grad_shift_ffn,
        ]
    )
    vec = jnp.concatenate([vec, grad_b_inner.reshape(4, model_dim)]).astype(jnp.bfloat16)
    for axis_name, bit in (("twin", 1), ("dp", 1), ("dp", 2)):
        vec = add_low(vec, swap(vec, axis_name, bit))
    vec = vec.astype(jnp.float32) + sum(
        swap(vec, "fsdp", s).astype(jnp.float32) for s in (1, 2, 3)
    )
    vec_small = lax.dynamic_slice(vec, (0, depth * shard), (8, shard))
    out_b_inner = lax.dynamic_index_in_dim(vec[8:], depth, 0, keepdims=False)

    outs = scatter_out(place, back_a, back_cb)
    return (
        output,
        grad_tokens,
        outs[0],
        vec_small[0],
        outs[1],
        outs[2],
        vec_small[1],
        outs[3],
        vec_small[2],
        vec_small[3],
        vec_small[4],
        outs[4],
        out_b_inner,
        outs[5],
        vec_small[5],
        vec_small[6],
        vec_small[7],
    )


def masked_scores(query, keys, seg_row):
    scores = jnp.einsum("qhd,khd->hqk", query, keys, preferred_element_type=jnp.float32) * HD ** (
        -0.5
    )
    same = seg_row[:, None] == seg_row[None, :]
    return jnp.where(same[None], scores, -1e30)


def attend_row(item):
    query, keys, values, seg_row = item
    scores = masked_scores(query, keys, seg_row)
    row_max = jnp.max(scores, axis=2, keepdims=True)
    exp_scores = jnp.exp(scores - row_max)
    row_sum = jnp.sum(exp_scores, axis=2, keepdims=True)
    attn_prob = (exp_scores / row_sum).astype(jnp.bfloat16)
    context = jnp.einsum("hqk,khd->qhd", attn_prob, values, preferred_element_type=jnp.float32)
    return (context.astype(jnp.bfloat16), row_max[:, :, 0] + jnp.log(row_sum[:, :, 0]))


def attend_row_back(item):
    query, keys, values, seg_row, log_total, grad_ctx = item
    attn_prob = jnp.exp(masked_scores(query, keys, seg_row) - log_total[:, :, None])
    grad_values = jnp.einsum(
        "hqk,qhd->khd", attn_prob.astype(jnp.bfloat16), grad_ctx, preferred_element_type=jnp.float32
    )
    grad_prob = jnp.einsum("qhd,khd->hqk", grad_ctx, values, preferred_element_type=jnp.float32)
    grad_scores = attn_prob * (grad_prob - jnp.sum(attn_prob * grad_prob, axis=2, keepdims=True))
    grad_scores = grad_scores.astype(jnp.bfloat16)
    grad_query = jnp.einsum(
        "hqk,khd->qhd", grad_scores, keys, preferred_element_type=jnp.float32
    ) * HD ** (-0.5)
    grad_keys = jnp.einsum(
        "hqk,qhd->khd", grad_scores, query, preferred_element_type=jnp.float32
    ) * HD ** (-0.5)
    return (
        grad_query.astype(jnp.bfloat16),
        grad_keys.astype(jnp.bfloat16),
        grad_values.astype(jnp.bfloat16),
    )


def forward_block(block_tok, seg_block, weights):
    (
        w_query,
        b_query,
        w_key,
        w_value,
        b_value,
        w_out,
        b_out,
        gain_attn,
        shift_attn,
        w_inner,
        b_inner,
        w_outer,
        b_outer,
        gain_ffn,
        shift_ffn,
    ) = weights
    row_count, seq_len, model_dim = block_tok.shape
    tok_flat = block_tok.reshape(row_count * seq_len, model_dim)
    head_shape = (row_count, seq_len, H, HD)
    query = (plain_dot(tok_flat, w_query) + b_query).astype(jnp.bfloat16).reshape(head_shape)
    keys = plain_dot(tok_flat, w_key).astype(jnp.bfloat16).reshape(head_shape)
    values = (plain_dot(tok_flat, w_value) + b_value).astype(jnp.bfloat16).reshape(head_shape)
    context, log_total = lax.map(attend_row, (query, keys, values, seg_block))
    context = context.reshape(row_count * seq_len, model_dim)
    normed_attn, inv_attn = normalize(
        tok_flat.astype(jnp.float32) + plain_dot(context, w_out) + b_out
    )
    mid_state = normed_attn * gain_attn + shift_attn
    mid_low = mid_state.astype(jnp.bfloat16)
    inner = plain_dot(mid_low, w_inner) + b_inner
    cdf_value, slope = gelu_parts(inner)
    activ = (inner * cdf_value).astype(jnp.bfloat16)
    normed_ffn, inv_ffn = normalize(mid_state + plain_dot(activ, w_outer) + b_outer)
    final = normed_ffn * gain_ffn + shift_ffn
    saved = (
        query,
        keys,
        values,
        log_total,
        context,
        normed_attn,
        inv_attn,
        mid_low,
        inner,
        activ,
        normed_ffn,
        inv_ffn,
    )
    return (final, saved)


def backward_block(grad_final, block_tok, seg_block, weights, saved):
    (
        w_query,
        b_query,
        w_key,
        w_value,
        b_value,
        w_out,
        b_out,
        gain_attn,
        shift_attn,
        w_inner,
        b_inner,
        w_outer,
        b_outer,
        gain_ffn,
        shift_ffn,
    ) = weights
    (
        query,
        keys,
        values,
        log_total,
        context,
        normed_attn,
        inv_attn,
        mid_low,
        inner,
        activ,
        normed_ffn,
        inv_ffn,
    ) = saved
    row_count, seq_len, model_dim = block_tok.shape
    tok_flat = block_tok.reshape(row_count * seq_len, model_dim)
    grad_gain_ffn = jnp.sum(grad_final * normed_ffn, axis=0)
    grad_shift_ffn = jnp.sum(grad_final, axis=0)
    grad_h2 = norm_back(grad_final * gain_ffn, normed_ffn, inv_ffn)
    grad_branch = grad_h2.astype(jnp.bfloat16)
    grad_w_outer = cross_dot(activ, grad_branch)
    grad_b_outer = jnp.sum(grad_branch, axis=0, dtype=jnp.float32)
    cdf_value, slope = gelu_parts(inner)
    grad_inner = (back_dot(grad_branch, w_outer) * slope).astype(jnp.bfloat16)
    grad_w_inner = cross_dot(mid_low, grad_inner)
    grad_b_inner = jnp.sum(grad_inner, axis=0, dtype=jnp.float32)
    grad_mid = grad_h2 + back_dot(grad_inner, w_inner)
    grad_gain_attn = jnp.sum(grad_mid * normed_attn, axis=0)
    grad_shift_attn = jnp.sum(grad_mid, axis=0)
    grad_h1 = norm_back(grad_mid * gain_attn, normed_attn, inv_attn)
    grad_attn = grad_h1.astype(jnp.bfloat16)
    grad_w_out = cross_dot(context, grad_attn)
    grad_b_out = jnp.sum(grad_attn, axis=0, dtype=jnp.float32)
    grad_ctx = back_dot(grad_attn, w_out).astype(jnp.bfloat16).reshape(row_count, seq_len, H, HD)
    grad_query, grad_keys, grad_values = lax.map(
        attend_row_back, (query, keys, values, seg_block, log_total, grad_ctx)
    )
    flat_shape = (row_count * seq_len, model_dim)
    grad_query = grad_query.reshape(flat_shape)
    grad_keys = grad_keys.reshape(flat_shape)
    grad_values = grad_values.reshape(flat_shape)
    grad_w_query = cross_dot(tok_flat, grad_query)
    grad_b_query = jnp.sum(grad_query, axis=0, dtype=jnp.float32)
    grad_w_key = cross_dot(tok_flat, grad_keys)
    grad_w_value = cross_dot(tok_flat, grad_values)
    grad_b_value = jnp.sum(grad_values, axis=0, dtype=jnp.float32)
    grad_tok = (
        grad_h1
        + back_dot(grad_query, w_query)
        + back_dot(grad_keys, w_key)
        + back_dot(grad_values, w_value)
    )
    grads = (
        grad_w_query,
        grad_b_query,
        grad_w_key,
        grad_w_value,
        grad_b_value,
        grad_w_out,
        grad_b_out,
        grad_gain_attn,
        grad_shift_attn,
        grad_w_inner,
        grad_b_inner,
        grad_w_outer,
        grad_b_outer,
        grad_gain_ffn,
        grad_shift_ffn,
    )
    return (grad_tok.astype(jnp.bfloat16).reshape(row_count, seq_len, model_dim), grads)


def reduce_grads(grads):
    (
        grad_w_query,
        grad_b_query,
        grad_w_key,
        grad_w_value,
        grad_b_value,
        grad_w_out,
        grad_b_out,
        grad_gain_attn,
        grad_shift_attn,
        grad_w_inner,
        grad_b_inner,
        grad_w_outer,
        grad_b_outer,
        grad_gain_ffn,
        grad_shift_ffn,
    ) = grads
    (
        shard_w_query,
        shard_b_query,
        shard_w_key,
        shard_w_value,
        shard_b_value,
        shard_w_out,
        shard_b_out,
        shard_gain_attn,
        shard_shift_attn,
        shard_w_inner,
        shard_b_inner,
        shard_w_outer,
        shard_b_outer,
        shard_gain_ffn,
        shard_shift_ffn,
    ) = (
        lax.psum_scatter(
            grad_w_query.astype(jnp.bfloat16), "fsdp", scatter_dimension=0, tiled=True
        ).astype(jnp.float32),
        lax.psum_scatter(
            grad_b_query.astype(jnp.bfloat16), "fsdp", scatter_dimension=0, tiled=True
        ).astype(jnp.float32),
        lax.psum_scatter(
            grad_w_key.astype(jnp.bfloat16), "fsdp", scatter_dimension=0, tiled=True
        ).astype(jnp.float32),
        lax.psum_scatter(
            grad_w_value.astype(jnp.bfloat16), "fsdp", scatter_dimension=0, tiled=True
        ).astype(jnp.float32),
        lax.psum_scatter(
            grad_b_value.astype(jnp.bfloat16), "fsdp", scatter_dimension=0, tiled=True
        ).astype(jnp.float32),
        lax.psum_scatter(
            grad_w_out.astype(jnp.bfloat16), "fsdp", scatter_dimension=0, tiled=True
        ).astype(jnp.float32),
        lax.psum_scatter(
            grad_b_out.astype(jnp.bfloat16), "fsdp", scatter_dimension=0, tiled=True
        ).astype(jnp.float32),
        lax.psum_scatter(
            grad_gain_attn.astype(jnp.bfloat16), "fsdp", scatter_dimension=0, tiled=True
        ).astype(jnp.float32),
        lax.psum_scatter(
            grad_shift_attn.astype(jnp.bfloat16), "fsdp", scatter_dimension=0, tiled=True
        ).astype(jnp.float32),
        lax.psum_scatter(
            grad_w_inner.astype(jnp.bfloat16), "fsdp", scatter_dimension=0, tiled=True
        ).astype(jnp.float32),
        lax.psum_scatter(
            grad_b_inner.astype(jnp.bfloat16), "fsdp", scatter_dimension=0, tiled=True
        ).astype(jnp.float32),
        lax.psum_scatter(
            grad_w_outer.astype(jnp.bfloat16), "fsdp", scatter_dimension=0, tiled=True
        ).astype(jnp.float32),
        lax.psum_scatter(
            grad_b_outer.astype(jnp.bfloat16), "fsdp", scatter_dimension=0, tiled=True
        ).astype(jnp.float32),
        lax.psum_scatter(
            grad_gain_ffn.astype(jnp.bfloat16), "fsdp", scatter_dimension=0, tiled=True
        ).astype(jnp.float32),
        lax.psum_scatter(
            grad_shift_ffn.astype(jnp.bfloat16), "fsdp", scatter_dimension=0, tiled=True
        ).astype(jnp.float32),
    )
    return (
        lax.psum(shard_w_query.astype(jnp.bfloat16), ("twin", "dp")).astype(jnp.float32),
        lax.psum(shard_b_query.astype(jnp.bfloat16), ("twin", "dp")).astype(jnp.float32),
        lax.psum(shard_w_key.astype(jnp.bfloat16), ("twin", "dp")).astype(jnp.float32),
        lax.psum(shard_w_value.astype(jnp.bfloat16), ("twin", "dp")).astype(jnp.float32),
        lax.psum(shard_b_value.astype(jnp.bfloat16), ("twin", "dp")).astype(jnp.float32),
        lax.psum(shard_w_out.astype(jnp.bfloat16), ("twin", "dp")).astype(jnp.float32),
        lax.psum(shard_b_out.astype(jnp.bfloat16), ("twin", "dp")).astype(jnp.float32),
        lax.psum(shard_gain_attn.astype(jnp.bfloat16), ("twin", "dp")).astype(jnp.float32),
        lax.psum(shard_shift_attn.astype(jnp.bfloat16), ("twin", "dp")).astype(jnp.float32),
        lax.psum(shard_w_inner.astype(jnp.bfloat16), ("twin", "dp")).astype(jnp.float32),
        lax.psum(shard_b_inner.astype(jnp.bfloat16), ("twin", "dp")).astype(jnp.float32),
        lax.psum(shard_w_outer.astype(jnp.bfloat16), ("twin", "dp")).astype(jnp.float32),
        lax.psum(shard_b_outer.astype(jnp.bfloat16), ("twin", "dp")).astype(jnp.float32),
        lax.psum(shard_gain_ffn.astype(jnp.bfloat16), ("twin", "dp")).astype(jnp.float32),
        lax.psum(shard_shift_ffn.astype(jnp.bfloat16), ("twin", "dp")).astype(jnp.float32),
    )


def general_device(
    tokens,
    w_query,
    b_query,
    w_key,
    w_value,
    b_value,
    w_out,
    b_out,
    gain_attn,
    shift_attn,
    w_inner,
    b_inner,
    w_outer,
    b_outer,
    gain_ffn,
    shift_ffn,
    lengths,
    labels,
):
    row_total, seq_len, model_dim = tokens.shape
    block_rows = row_total // MB
    seg_all = segment_ids(lengths, seq_len)
    member = (seg_all[:, None, :] == jnp.arange(SEG, dtype=jnp.int32)[None, :, None]).astype(
        jnp.float32
    )
    counts = lengths[:, :SEG].astype(jnp.float32)
    finals = []
    saved_list = []
    for block_idx in range(MB):
        row_span = slice(block_idx * block_rows, (block_idx + 1) * block_rows)
        weights = (
            lax.all_gather(w_query, "fsdp", axis=0, tiled=True),
            lax.all_gather(b_query, "fsdp", axis=0, tiled=True),
            lax.all_gather(w_key, "fsdp", axis=0, tiled=True),
            lax.all_gather(w_value, "fsdp", axis=0, tiled=True),
            lax.all_gather(b_value, "fsdp", axis=0, tiled=True),
            lax.all_gather(w_out, "fsdp", axis=0, tiled=True),
            lax.all_gather(b_out, "fsdp", axis=0, tiled=True),
            lax.all_gather(gain_attn, "fsdp", axis=0, tiled=True),
            lax.all_gather(shift_attn, "fsdp", axis=0, tiled=True),
            lax.all_gather(w_inner, "fsdp", axis=0, tiled=True),
            lax.all_gather(b_inner, "fsdp", axis=0, tiled=True),
            lax.all_gather(w_outer, "fsdp", axis=0, tiled=True),
            lax.all_gather(b_outer, "fsdp", axis=0, tiled=True),
            lax.all_gather(gain_ffn, "fsdp", axis=0, tiled=True),
            lax.all_gather(shift_ffn, "fsdp", axis=0, tiled=True),
        )
        final, saved = forward_block(tokens[row_span], seg_all[row_span], weights)
        finals.append(final.reshape(block_rows, seq_len, model_dim))
        saved_list.append(saved)
    final_all = jnp.concatenate(finals, axis=0)
    pooled_f = (
        jnp.einsum("rst,rtd->rsd", member, final_all, precision=lax.Precision.HIGHEST)
        / counts[:, :, None]
    )
    pooled_low = pooled_f.reshape(row_total * SEG, model_dim).astype(jnp.bfloat16)
    gathered = lax.all_gather(pooled_low, ("twin", "dp", "fsdp"), axis=0, tiled=True)
    own_count = pooled_low.shape[0]
    half_count = labels.shape[0]
    twin_side = lax.axis_index("twin")
    device = lax.axis_index(("twin", "dp", "fsdp"))
    first_seg = device * own_count
    other_start = (1 - twin_side) * half_count
    other_side = lax.dynamic_slice_in_dim(gathered, other_start, half_count, 0)
    own_f = pooled_low.astype(jnp.float32)
    other_f = other_side.astype(jnp.float32)
    inv_own = lax.rsqrt(jnp.sum(own_f * own_f, axis=1) + pool_eps)
    inv_other = lax.rsqrt(jnp.sum(other_f * other_f, axis=1) + pool_eps)
    col_index = jnp.arange(half_count, dtype=jnp.int32)
    similar = sim_scale * back_dot(pooled_low, other_side) * inv_own[:, None] * inv_other[None, :]
    own_labels = lax.dynamic_slice_in_dim(
        labels, jnp.minimum(first_seg, half_count - own_count), own_count, 0
    )
    own_index = first_seg - half_count + jnp.arange(own_count, dtype=jnp.int32)
    target = jnp.where(
        twin_side == 0,
        col_index[None, :] == own_labels[:, None],
        labels[None, :] == own_index[:, None],
    ).astype(jnp.float32)
    row_max = jnp.max(similar, axis=1, keepdims=True)
    log_total = row_max[:, 0] + jnp.log(jnp.sum(jnp.exp(similar - row_max), axis=1))
    grad_sim = jnp.exp(similar - log_total[:, None]) - target
    weighted = grad_sim * similar
    grad_raw = sim_scale * grad_sim * inv_own[:, None] * inv_other[None, :]
    grad_own = (
        jnp.dot(grad_raw, other_f, precision=lax.Precision.HIGHEST)
        - (jnp.sum(weighted, axis=1) * inv_own * inv_own)[:, None] * own_f
    )
    grad_other = (
        lax.dot_general(grad_raw, own_f, (((0,), (0,)), ((), ())), precision=lax.Precision.HIGHEST)
        - (jnp.sum(weighted, axis=0) * inv_other * inv_other)[:, None] * other_f
    )
    term = jnp.zeros((2 * half_count, model_dim), jnp.float32)
    term = lax.dynamic_update_slice_in_dim(term, grad_other, other_start, 0)
    term = lax.dynamic_update_slice_in_dim(term, grad_own, first_seg, 0)
    grad_pooled = lax.psum_scatter(term, ("twin", "dp", "fsdp"), scatter_dimension=0, tiled=True)
    grad_scaled = grad_pooled.reshape(row_total, SEG, model_dim) / counts[:, :, None]
    grad_toks = []
    grad_total = None
    for block_idx in range(MB):
        row_span = slice(block_idx * block_rows, (block_idx + 1) * block_rows)
        weights = (
            lax.all_gather(w_query, "fsdp", axis=0, tiled=True),
            lax.all_gather(b_query, "fsdp", axis=0, tiled=True),
            lax.all_gather(w_key, "fsdp", axis=0, tiled=True),
            lax.all_gather(w_value, "fsdp", axis=0, tiled=True),
            lax.all_gather(b_value, "fsdp", axis=0, tiled=True),
            lax.all_gather(w_out, "fsdp", axis=0, tiled=True),
            lax.all_gather(b_out, "fsdp", axis=0, tiled=True),
            lax.all_gather(gain_attn, "fsdp", axis=0, tiled=True),
            lax.all_gather(shift_attn, "fsdp", axis=0, tiled=True),
            lax.all_gather(w_inner, "fsdp", axis=0, tiled=True),
            lax.all_gather(b_inner, "fsdp", axis=0, tiled=True),
            lax.all_gather(w_outer, "fsdp", axis=0, tiled=True),
            lax.all_gather(b_outer, "fsdp", axis=0, tiled=True),
            lax.all_gather(gain_ffn, "fsdp", axis=0, tiled=True),
            lax.all_gather(shift_ffn, "fsdp", axis=0, tiled=True),
        )
        grad_final = jnp.einsum(
            "rst,rsd->rtd", member[row_span], grad_scaled[row_span], precision=lax.Precision.HIGHEST
        ).reshape(block_rows * seq_len, model_dim)
        grad_tok, grads = backward_block(
            grad_final, tokens[row_span], seg_all[row_span], weights, saved_list[block_idx]
        )
        grad_toks.append(grad_tok)
        grads = reduce_grads(grads)
        grad_total = grads if grad_total is None else jax.tree.map(jnp.add, grad_total, grads)
    output = final_all.astype(jnp.bfloat16)
    grad_tokens = jnp.concatenate(grad_toks, axis=0)
    return (output, grad_tokens) + tuple(grad_total)


def solution(mesh):
    placed = (
        P(("twin", "dp", "fsdp"), None, None),
        P("fsdp", None),
        P("fsdp"),
        P("fsdp", None),
        P("fsdp", None),
        P("fsdp"),
        P("fsdp", None),
        P("fsdp"),
        P("fsdp"),
        P("fsdp"),
        P("fsdp", None),
        P("fsdp"),
        P("fsdp", None),
        P("fsdp"),
        P("fsdp"),
        P("fsdp"),
        P(("twin", "dp", "fsdp"), None),
        P(),
    )
    sizes = (mesh.shape["twin"], mesh.shape["dp"], mesh.shape["fsdp"])
    return jax.shard_map(
        per_device if sizes == (2, 4, 4) else general_device,
        mesh=mesh,
        in_specs=placed,
        out_specs=(
            P(("twin", "dp", "fsdp"), None, None),
            P(("twin", "dp", "fsdp"), None, None),
            P("fsdp", None),
            P("fsdp"),
            P("fsdp", None),
            P("fsdp", None),
            P("fsdp"),
            P("fsdp", None),
            P("fsdp"),
            P("fsdp"),
            P("fsdp"),
            P("fsdp", None),
            P("fsdp"),
            P("fsdp", None),
            P("fsdp"),
            P("fsdp"),
            P("fsdp"),
        ),
        check_vma=False,
    )
```

```python
import jax
import jax.numpy as jnp
from jax import lax
from jax.experimental import pallas as pl
from jax.experimental.pallas import tpu as pltpu
from jax.sharding import PartitionSpec as P

H = 12
HD = 64
SEG = 8
MB = 2
TQ = 128


norm_eps = 1e-12
pool_eps = 1e-06
sim_scale = 20.0


def cross_dot(left, right):
    return lax.dot_general(
        left, right, (((0,), (0,)), ((), ())), preferred_element_type=jnp.float32
    )


def back_dot(left, right):
    return lax.dot_general(
        left, right, (((1,), (1,)), ((), ())), preferred_element_type=jnp.float32
    )


def plain_dot(left, right):
    return jnp.dot(left, right, preferred_element_type=jnp.float32)


def segment_ids(lengths, seq_len):
    ends = jnp.cumsum(lengths, axis=1, dtype=jnp.int32)
    position = jnp.arange(seq_len, dtype=jnp.int32)
    return jnp.sum((position[None, :, None] >= ends[:, None, :]).astype(jnp.int32), axis=2)


def normalize(hidden):
    centred = hidden - jnp.mean(hidden, axis=-1, keepdims=True)
    inv_dev = lax.rsqrt(jnp.mean(centred * centred, axis=-1, keepdims=True) + norm_eps)
    return (centred * inv_dev, inv_dev)


def norm_back(grad_normed, normed, inv_dev):
    return inv_dev * (
        grad_normed
        - jnp.mean(grad_normed, axis=-1, keepdims=True)
        - normed * jnp.mean(grad_normed * normed, axis=-1, keepdims=True)
    )


def gelu_parts(inner):
    cdf_value = 0.5 * (1.0 + lax.erf(inner * 0.7071067811865476))
    slope = cdf_value + inner * jnp.exp(-0.5 * inner * inner) * 0.3989422804014327
    return (cdf_value, slope)


def key_span(tile, seq_len):
    return max(0, (tile - 1) * TQ), min(seq_len, (tile + 2) * TQ)


def split_heads(block):
    lane = lax.broadcasted_iota(jnp.int32, block.shape, 1)
    zero = jnp.zeros_like(block)
    return jnp.concatenate(
        [jnp.where(lane < HD, block, zero), jnp.where(lane < HD, zero, block)], axis=0
    )


def merge_heads(double):
    count = double.shape[0] // 2
    lane = lax.broadcasted_iota(jnp.int32, (count, double.shape[1]), 1)
    return jnp.where(lane < HD, double[:count], double[count:])


def fill_bias(seg_col_ref, seg_row_ref, bias_ref, seq_len):
    for tile in range(seq_len // TQ):
        low, high = key_span(tile, seq_len)
        same = seg_col_ref[low:high, :] == seg_row_ref[:, tile * TQ : (tile + 1) * TQ]
        bias_ref[tile, : high - low, :] = jnp.where(same, 0.0, -1e30)


def attend_kernel(seg_col_ref, seg_row_ref, tok_ref, qkv_ref, ctx_ref, log_ref, bias_ref):
    seq_len = tok_ref.shape[0]

    @pl.when(pl.program_id(1) == 0)
    def _():
        fill_bias(seg_col_ref, seg_row_ref, bias_ref, seq_len)

    ctx_ref[0] = tok_ref[...]
    for tile in range(seq_len // TQ):
        low, high = key_span(tile, seq_len)
        rows = slice(tile * TQ, (tile + 1) * TQ)
        query = split_heads(qkv_ref[0, rows, :] * jnp.bfloat16(HD**-0.5))
        bias = bias_ref[tile, : high - low, :]
        scores = back_dot(qkv_ref[1, low:high, :], query) + jnp.concatenate([bias, bias], axis=1)
        top = jnp.max(scores, axis=0, keepdims=True)
        exp_scores = jnp.exp(scores - top)
        row_sum = jnp.sum(exp_scores, axis=0, keepdims=True)
        prob = (exp_scores * (1.0 / row_sum)).astype(jnp.bfloat16)
        context = cross_dot(prob, qkv_ref[2, low:high, :])
        ctx_ref[1, rows, :] = merge_heads(context).astype(jnp.bfloat16)
        log_ref[0, 0, tile : tile + 1, :] = top + jnp.log(row_sum)


def attend_back_kernel(
    seg_col_ref, seg_row_ref, qkv_ref, grad_ref, log_ref, attn_ref, out_ref, bias_ref, key_acc, val_acc
):
    seq_len = attn_ref.shape[0]

    @pl.when(pl.program_id(1) == 0)
    def _():
        fill_bias(seg_col_ref, seg_row_ref, bias_ref, seq_len)

    key_acc[...] = jnp.zeros_like(key_acc)
    val_acc[...] = jnp.zeros_like(val_acc)
    out_ref[3] = attn_ref[...]
    for tile in range(seq_len // TQ):
        low, high = key_span(tile, seq_len)
        rows = slice(tile * TQ, (tile + 1) * TQ)
        query = split_heads(qkv_ref[0, rows, :] * jnp.bfloat16(HD**-0.5))
        grad = split_heads(grad_ref[rows, :])
        bias = bias_ref[tile, : high - low, :]
        keys = qkv_ref[1, low:high, :]
        scores = back_dot(keys, query) + jnp.concatenate([bias, bias], axis=1)
        prob = jnp.exp(scores - log_ref[0, 0, tile : tile + 1, :])
        grad_prob = back_dot(qkv_ref[2, low:high, :], grad)
        total = jnp.sum(prob * grad_prob, axis=0, keepdims=True)
        grad_scores = (prob * (grad_prob - total)).astype(jnp.bfloat16)
        val_acc[low:high, :] += plain_dot(prob.astype(jnp.bfloat16), grad)
        key_acc[low:high, :] += plain_dot(grad_scores, query)
        grad_query = merge_heads(cross_dot(grad_scores, keys))
        out_ref[0, rows, :] = (grad_query * HD**-0.5).astype(jnp.bfloat16)
    out_ref[1] = key_acc[...].astype(jnp.bfloat16)
    out_ref[2] = val_acc[...].astype(jnp.bfloat16)


def attend(seg_all, tok_flat, qkv):
    row_count, seq_len = seg_all.shape
    token_count, model_dim = tok_flat.shape
    pairs = model_dim // (2 * HD)
    tiles = seq_len // TQ
    return pl.pallas_call(
        attend_kernel,
        grid=(row_count, pairs),
        in_specs=[
            pl.BlockSpec((None, seq_len, 1), lambda r, p: (r, 0, 0)),
            pl.BlockSpec((None, 1, seq_len), lambda r, p: (r, 0, 0)),
            pl.BlockSpec((seq_len, 2 * HD), lambda r, p: (r, p)),
            pl.BlockSpec((3, seq_len, 2 * HD), lambda r, p: (0, r, p)),
        ],
        out_specs=[
            pl.BlockSpec((2, seq_len, 2 * HD), lambda r, p: (0, r, p)),
            pl.BlockSpec((1, 1, tiles, 2 * TQ), lambda r, p: (r, p, 0, 0)),
        ],
        out_shape=[
            jax.ShapeDtypeStruct((2, token_count, model_dim), jnp.bfloat16),
            jax.ShapeDtypeStruct((row_count, pairs, tiles, 2 * TQ), jnp.float32),
        ],
        scratch_shapes=[pltpu.VMEM((tiles, 3 * TQ, TQ), jnp.float32)],
        cost_estimate=pl.CostEstimate(
            flops=4 * token_count * 3 * TQ * model_dim * 2,
            bytes_accessed=token_count * model_dim * 14,
            transcendentals=token_count * 3 * TQ * 2 * pairs,
        ),
        name="attend",
    )(seg_all[:, :, None], seg_all[:, None, :], tok_flat, qkv)


def attend_back(seg_all, qkv, grad_ctx, log_total, grad_attn):
    row_count, seq_len = seg_all.shape
    token_count, model_dim = grad_ctx.shape
    pairs = model_dim // (2 * HD)
    tiles = seq_len // TQ
    flat = pl.BlockSpec((seq_len, 2 * HD), lambda r, p: (r, p))
    return pl.pallas_call(
        attend_back_kernel,
        grid=(row_count, pairs),
        in_specs=[
            pl.BlockSpec((None, seq_len, 1), lambda r, p: (r, 0, 0)),
            pl.BlockSpec((None, 1, seq_len), lambda r, p: (r, 0, 0)),
            pl.BlockSpec((3, seq_len, 2 * HD), lambda r, p: (0, r, p)),
            flat,
            pl.BlockSpec((1, 1, tiles, 2 * TQ), lambda r, p: (r, p, 0, 0)),
            flat,
        ],
        out_specs=pl.BlockSpec((4, seq_len, 2 * HD), lambda r, p: (0, r, p)),
        out_shape=jax.ShapeDtypeStruct((4, token_count, model_dim), jnp.bfloat16),
        scratch_shapes=[
            pltpu.VMEM((tiles, 3 * TQ, TQ), jnp.float32),
            pltpu.VMEM((seq_len, 2 * HD), jnp.float32),
            pltpu.VMEM((seq_len, 2 * HD), jnp.float32),
        ],
        cost_estimate=pl.CostEstimate(
            flops=10 * token_count * 3 * TQ * model_dim * 2,
            bytes_accessed=token_count * model_dim * 20,
            transcendentals=token_count * 3 * TQ * 2 * pairs,
        ),
        name="attend_back",
    )(seg_all[:, :, None], seg_all[:, None, :], qkv, grad_ctx, log_total, grad_attn)


def swap(value, axis_name, bit):
    count = 2 if axis_name == "twin" else 4
    return lax.ppermute(value, axis_name, [(i, i ^ bit) for i in range(count)])


def hold(values):
    return lax.optimization_barrier(values)


def across_depth(piece):
    return jnp.stack([swap(piece, "fsdp", s) for s in (1, 2, 3)])


def assemble_wide_kernel(place_ref, *refs):
    step = pl.program_id(0)
    out_ref = refs[-1]
    count = len(refs) - 3
    near_ref, far_ref = refs[count], refs[count + 1]
    model_dim = near_ref.shape[-1]
    half = near_ref.shape[-2]

    @pl.when(step == 0)
    def _():
        if count == 1:
            out_ref[...] = refs[0][...]
        else:
            for index in range(count):
                out_ref[:, index * model_dim : (index + 1) * model_dim] = refs[index][...]

    @pl.when(step > 0)
    def _():
        for index in range(8):
            spot = place_ref[1] ^ index
            source = near_ref if index < 4 else far_ref
            row = pl.multiple_of((spot % 2) * half, half)
            column = pl.multiple_of((spot // 2) * model_dim, model_dim)
            out_ref[pl.ds(row, half), pl.ds(column, model_dim)] = source[index % 4]


def assemble_tall_kernel(place_ref, shard_ref, near_ref, far_ref, out_ref):
    step = pl.program_id(0)
    half = near_ref.shape[-2]

    @pl.when(step == 0)
    def _():
        out_ref[...] = shard_ref[...]

    @pl.when(step > 0)
    def _():
        for index in range(8):
            source = near_ref if index < 4 else far_ref
            row = pl.multiple_of((place_ref[1] ^ index) * half, half)
            out_ref[pl.ds(row, half), :] = source[index % 4]


def assemble(kernel, place, shards, near, far, part, name):
    rows = shards[0].shape[0]
    columns = sum(shard.shape[1] for shard in shards)
    half, model_dim = near.shape[-2:]
    gathered = pl.BlockSpec(
        (4, None, None, half, model_dim),
        lambda s, place: (0, jnp.maximum(s - 1, 0), part, 0, 0),
    )
    return pl.pallas_call(
        kernel,
        grid_spec=pltpu.PrefetchScalarGridSpec(
            num_scalar_prefetch=1,
            grid=(4,),
            in_specs=[pl.BlockSpec(shard.shape, lambda s, place: (0, 0)) for shard in shards]
            + [gathered, gathered],
            out_specs=pl.BlockSpec((rows, columns), lambda s, place: (place[0] ^ s, 0)),
        ),
        out_shape=jax.ShapeDtypeStruct((4 * rows, columns), jnp.bfloat16),
        cost_estimate=pl.CostEstimate(
            flops=0, bytes_accessed=16 * rows * columns, transcendentals=0
        ),
        name=name,
    )(place, *shards, near, far)


def project_kernel(tok_ref, weight_ref, bias_ref, out_ref):
    out_ref[...] = (plain_dot(tok_ref[...], weight_ref[...]) + bias_ref[0]).astype(jnp.bfloat16)


def project(tok_flat, square, biases):
    token_count, model_dim = tok_flat.shape
    return pl.pallas_call(
        project_kernel,
        grid=(3,),
        in_specs=[
            pl.BlockSpec((token_count, model_dim), lambda m: (0, 0)),
            pl.BlockSpec((model_dim, model_dim), lambda m: (0, m)),
            pl.BlockSpec((1, 1, model_dim), lambda m: (m, 0, 0)),
        ],
        out_specs=pl.BlockSpec((None, token_count, model_dim), lambda m: (m, 0, 0)),
        out_shape=jax.ShapeDtypeStruct((3, token_count, model_dim), jnp.bfloat16),
        cost_estimate=pl.CostEstimate(
            flops=6 * token_count * model_dim**2,
            bytes_accessed=8 * token_count * model_dim,
            transcendentals=0,
        ),
        name="project",
    )(tok_flat, square, biases)


def project_back_kernel(grad_ref, weight_ref, base_ref, out_ref, acc_ref):
    step = pl.program_id(0)

    @pl.when(step == 0)
    def _():
        acc_ref[...] = base_ref[...]

    acc_ref[...] += back_dot(grad_ref[...], weight_ref[...])

    @pl.when(step == 2)
    def _():
        out_ref[...] = acc_ref[...].astype(jnp.bfloat16)


def project_back(grads, square, base):
    _, token_count, model_dim = grads.shape
    return pl.pallas_call(
        project_back_kernel,
        grid=(3,),
        in_specs=[
            pl.BlockSpec((None, token_count, model_dim), lambda m: (m, 0, 0)),
            pl.BlockSpec((model_dim, model_dim), lambda m: (0, m)),
            pl.BlockSpec((token_count, model_dim), lambda m: (0, 0)),
        ],
        out_specs=pl.BlockSpec((token_count, model_dim), lambda m: (0, 0)),
        out_shape=jax.ShapeDtypeStruct((token_count, model_dim), jnp.bfloat16),
        scratch_shapes=[pltpu.VMEM((token_count, model_dim), jnp.float32)],
        cost_estimate=pl.CostEstimate(
            flops=6 * token_count * model_dim**2,
            bytes_accessed=8 * token_count * model_dim,
            transcendentals=0,
        ),
        name="project_back",
    )(grads, square, base)


def weight_grad_kernel(place_ref, left_ref, right_ref, out_ref, acc_ref):
    acc_ref[...] = cross_dot(left_ref[...], right_ref[...])
    half = out_ref.shape[-2]
    for x in range(2):
        for z in range(4):
            row = pl.multiple_of(
                ((place_ref[0] ^ z) * 2 + ((place_ref[1] ^ x) % 2)) * half, half
            )
            out_ref[x, z] = acc_ref[pl.ds(row, half), :].astype(jnp.bfloat16)


def weight_grad_tall_kernel(place_ref, left_ref, right_ref, out_ref, acc_ref):
    acc_ref[...] = cross_dot(left_ref[...], right_ref[...])
    half = out_ref.shape[-2]
    for index in range(4):
        row = pl.multiple_of(((place_ref[1] ^ index) % 4) * half, half)
        out_ref[index // 2, index % 2] = acc_ref[pl.ds(row, half), :].astype(jnp.bfloat16)


def weight_grad(kind, side, place, left, right):
    token_count = left.shape[-2]
    model_dim = left.shape[-1] if kind != "tall" else right.shape[-1]
    half = model_dim // 8
    block = lambda y, place: (place[1] // 2) ^ (2 * side + y)
    if kind == "square":
        left_spec = pl.BlockSpec(
            (None, token_count, model_dim), lambda y, place: (block(y, place) // 3, 0, 0)
        )
        right_spec = pl.BlockSpec(
            (None, token_count, model_dim), lambda y, place: (block(y, place), 0, 0)
        )
    elif kind == "wide":
        left_spec = pl.BlockSpec((token_count, model_dim), lambda y, place: (0, 0))
        right_spec = pl.BlockSpec((token_count, model_dim), lambda y, place: (0, block(y, place)))
    if kind == "tall":
        return pl.pallas_call(
            weight_grad_tall_kernel,
            grid_spec=pltpu.PrefetchScalarGridSpec(
                num_scalar_prefetch=1,
                grid=(4,),
                in_specs=[
                    pl.BlockSpec(
                        (token_count, model_dim // 2),
                        lambda z, place: (0, (place[0] ^ z) * 2 + ((place[1] // 4) ^ side)),
                    ),
                    pl.BlockSpec((token_count, model_dim), lambda z, place: (0, 0)),
                ],
                out_specs=pl.BlockSpec(
                    (2, 2, None, half, model_dim), lambda z, place: (0, 0, z, 0, 0)
                ),
                scratch_shapes=[pltpu.VMEM((model_dim // 2, model_dim), jnp.float32)],
            ),
            out_shape=jax.ShapeDtypeStruct((2, 2, 4, half, model_dim), jnp.bfloat16),
            cost_estimate=pl.CostEstimate(
                flops=4 * token_count * model_dim**2,
                bytes_accessed=8 * token_count * model_dim,
                transcendentals=0,
            ),
            name="weight_grad_tall",
        )(place, left, right)
    return pl.pallas_call(
        weight_grad_kernel,
        grid_spec=pltpu.PrefetchScalarGridSpec(
            num_scalar_prefetch=1,
            grid=(2,),
            in_specs=[left_spec, right_spec],
            out_specs=pl.BlockSpec(
                (None, 2, 4, half, model_dim), lambda y, place: (y, 0, 0, 0, 0)
            ),
            scratch_shapes=[pltpu.VMEM((model_dim, model_dim), jnp.float32)],
        ),
        out_shape=jax.ShapeDtypeStruct((2, 2, 4, half, model_dim), jnp.bfloat16),
        cost_estimate=pl.CostEstimate(
            flops=4 * token_count * model_dim**2,
            bytes_accessed=8 * token_count * model_dim,
            transcendentals=0,
        ),
        name="weight_grad_" + kind,
    )(place, left, right)


def add_low(*parts):
    total = parts[0].astype(jnp.float32)
    for part in parts[1:]:
        total = total + part.astype(jnp.float32)
    return total.astype(jnp.bfloat16)


def gather_back(piece):
    pair = jnp.stack([piece, swap(piece, "dp", 1)])
    quad = jnp.concatenate([pair, swap(pair, "dp", 2)])
    return quad, swap(quad, "twin", 1)


def scatter_out_kernel(place_ref, quad_a, far_a, quad_b, far_b, *outs):
    half, model_dim = quad_a.shape[-2:]
    for index in range(8):
        spot = place_ref[1] ^ index
        pick = lambda near, far: (near if index < 4 else far)[index % 4]
        value = pick(quad_a, far_a).astype(jnp.float32)
        row = pl.multiple_of((spot % 2) * half, half)
        for matrix in range(4):

            @pl.when(spot // 2 == matrix)
            def _():
                outs[matrix][pl.ds(row, half), :] = value

        column = pl.multiple_of((spot // 2) * model_dim, model_dim)
        both = pick(quad_b, far_b)
        outs[4][pl.ds(row, half), pl.ds(column, model_dim)] = both[1].astype(jnp.float32)
        tall_row = pl.multiple_of(spot * half, half)
        outs[5][pl.ds(tall_row, half), :] = both[0].astype(jnp.float32)


def scatter_out(place, gathered_a, gathered_b):
    half, model_dim = gathered_a[0].shape[-2:]
    shard = 2 * half
    whole = pl.BlockSpec(memory_space=pltpu.VMEM)
    shapes = [(shard, model_dim)] * 4 + [(shard, 4 * model_dim), (4 * shard, model_dim)]
    return pl.pallas_call(
        scatter_out_kernel,
        in_specs=[pl.BlockSpec(memory_space=pltpu.SMEM)] + [whole] * 4,
        out_specs=[whole] * 6,
        out_shape=[jax.ShapeDtypeStruct(shape, jnp.float32) for shape in shapes],
        name="scatter_out",
    )(place, *gathered_a, *gathered_b)


def loss_grad(pooled_low, labels):
    own_count, model_dim = pooled_low.shape
    half_count = labels.shape[0]
    same = jnp.stack([pooled_low, swap(pooled_low, "dp", 1)])
    same = jnp.concatenate([same, swap(same, "dp", 2)])
    same = jnp.stack([same] + [swap(same, "fsdp", s) for s in (1, 2, 3)])
    same = same.reshape(half_count, model_dim)
    other = swap(same, "twin", 1)
    twin_side = lax.axis_index("twin")
    group, depth = lax.axis_index("dp"), lax.axis_index("fsdp")
    first = (group * 4 + depth) * own_count
    offset = jnp.arange(4, dtype=jnp.int32)
    numbers = ((offset[None, :] ^ group) * 4 + (offset[:, None] ^ depth)).reshape(16)
    numbers = (
        numbers[:, None] * own_count + jnp.arange(own_count, dtype=jnp.int32)[None, :]
    ).reshape(half_count)
    own_f = pooled_low.astype(jnp.float32)
    same_f = same.astype(jnp.float32)
    other_f = other.astype(jnp.float32)
    inv_own = lax.rsqrt(jnp.sum(own_f * own_f, axis=1) + pool_eps)
    inv_same = lax.rsqrt(jnp.sum(same_f * same_f, axis=1) + pool_eps)
    inv_other = lax.rsqrt(jnp.sum(other_f * other_f, axis=1) + pool_eps)
    similar = sim_scale * back_dot(same, other) * inv_same[:, None] * inv_other[None, :]
    col_max = jnp.max(similar, axis=0, keepdims=True)
    col_log = col_max[0] + jnp.log(jnp.sum(jnp.exp(similar - col_max), axis=0))
    own_sim = similar[:own_count]
    row_max = jnp.max(own_sim, axis=1, keepdims=True)
    row_log = row_max[:, 0] + jnp.log(jnp.sum(jnp.exp(own_sim - row_max), axis=1))
    own_labels = lax.dynamic_slice_in_dim(labels, first, own_count, 0)
    own_index = first + jnp.arange(own_count, dtype=jnp.int32)
    other_labels = labels[numbers]
    target = jnp.where(
        twin_side == 0,
        numbers[None, :] == own_labels[:, None],
        other_labels[None, :] == own_index[:, None],
    ).astype(jnp.float32)
    grad_sim = (
        jnp.exp(own_sim - row_log[:, None]) + jnp.exp(own_sim - col_log[None, :]) - 2.0 * target
    )
    grad_raw = sim_scale * grad_sim * inv_own[:, None] * inv_other[None, :]
    return (
        jnp.dot(grad_raw, other_f, precision=lax.Precision.HIGHEST)
        - (jnp.sum(grad_sim * own_sim, axis=1) * inv_own * inv_own)[:, None] * own_f
    )


def per_device(
    tokens,
    w_query,
    b_query,
    w_key,
    w_value,
    b_value,
    w_out,
    b_out,
    gain_attn,
    shift_attn,
    w_inner,
    b_inner,
    w_outer,
    b_outer,
    gain_ffn,
    shift_ffn,
    lengths,
    labels,
):
    row_total, seq_len, model_dim = tokens.shape
    token_count = row_total * seq_len
    shard = w_query.shape[0]
    half = shard // 2
    inner_dim = w_inner.shape[1]
    eighth = lax.axis_index("twin") * 4 + lax.axis_index("dp")
    depth = lax.axis_index("fsdp")
    place = jnp.stack([depth, eighth]).astype(jnp.int32)
    tok_flat = tokens.reshape(token_count, model_dim)

    stacked = jnp.stack([w_query, w_key, w_value, w_out]).reshape(8, half, model_dim)
    piece_a = lax.dynamic_index_in_dim(stacked, eighth, 0)
    piece_b = lax.dynamic_slice(
        w_inner, ((eighth % 2) * half, (eighth // 2) * model_dim), (half, model_dim)
    )
    piece_c = lax.dynamic_slice_in_dim(w_outer, eighth * half, half, 0)
    vectors = jnp.stack(
        [b_query, b_value, b_out, gain_attn, shift_attn, b_outer, gain_ffn, shift_ffn]
    )
    vectors = jnp.concatenate([vectors.reshape(8 * shard), b_inner])
    around = [vectors] + [swap(vectors, "fsdp", s) for s in (1, 2, 3)]
    ordered = jnp.stack(
        [sum(jnp.where(depth == z ^ s, around[s], 0) for s in range(4)) for z in range(4)]
    ).astype(jnp.float32)
    small = ordered[:, : 8 * shard].reshape(4, 8, shard).swapaxes(0, 1).reshape(8, model_dim)
    full_b_inner = ordered[:, 8 * shard :].reshape(inner_dim)
    seg_all = segment_ids(lengths, seq_len)
    member = (seg_all[:, None, :] == jnp.arange(SEG, dtype=jnp.int32)[None, :, None]).astype(
        jnp.float32
    )
    counts = lengths[:, :SEG].astype(jnp.float32)
    own_a = across_depth(piece_a)
    own_a, piece_bc, small, full_b_inner, seg_all, member = hold(
        (own_a, jnp.stack([piece_b, piece_c]), small, full_b_inner, seg_all, member)
    )
    beside_a, above_a = swap(own_a, "dp", 1), swap(own_a, "dp", 2)
    own_b = across_depth(piece_bc)
    beside_a, above_a, own_b = hold((beside_a, above_a, own_b))
    near_a = jnp.stack([own_a, beside_a, above_a, swap(beside_a, "dp", 2)])
    beside_b, above_b = swap(own_b, "dp", 1), swap(own_b, "dp", 2)
    far_a = swap(near_a, "twin", 1)
    b_query, b_value, b_out, gain_attn, shift_attn, b_outer, gain_ffn, shift_ffn = small
    biases = jnp.stack([b_query, jnp.zeros_like(b_query), b_value])[:, None]
    square = assemble(
        assemble_wide_kernel, place, [w_query, w_key, w_value, w_out], near_a, far_a, 0, "assemble_a"
    )
    full_w_out = square[:, 3 * model_dim :]
    qkv = project(tok_flat, square, biases)
    qkv, beside_b, above_b = hold((qkv, beside_b, above_b))
    corner_b = jnp.concatenate(
        [swap(beside_b[:, :1], "dp", 2), swap(above_b[:, 1:], "dp", 1)], axis=1
    )
    tok_ctx, log_total = attend(seg_all, tok_flat, qkv)
    tok_ctx, log_total, corner_b = hold((tok_ctx, log_total, corner_b))
    near_b = jnp.stack([own_b, beside_b, above_b, corner_b])
    far_b = swap(near_b, "twin", 1)
    wide = assemble(assemble_wide_kernel, place, [w_inner], near_b, far_b, 0, "assemble_b")
    tall = assemble(assemble_tall_kernel, place, [w_outer], near_b, far_b, 1, "assemble_c")
    context = tok_ctx[1]
    normed_attn, inv_attn = normalize(
        tok_flat.astype(jnp.float32) + plain_dot(context, full_w_out) + b_out
    )
    mid_state = normed_attn * gain_attn + shift_attn
    mid_low = mid_state.astype(jnp.bfloat16)
    inner = plain_dot(mid_low, wide) + full_b_inner
    cdf_value, slope = gelu_parts(inner)
    activ = (inner * cdf_value).astype(jnp.bfloat16)
    normed_ffn, inv_ffn = normalize(mid_state + plain_dot(activ, tall) + b_outer)
    final = normed_ffn * gain_ffn + shift_ffn
    output = final.astype(jnp.bfloat16).reshape(row_total, seq_len, model_dim)
    pooled_f = (
        jnp.einsum(
            "rst,rtd->rsd",
            member,
            final.reshape(row_total, seq_len, model_dim),
            precision=lax.Precision.HIGHEST,
        )
        / counts[:, :, None]
    )
    pooled_low = pooled_f.reshape(row_total * SEG, model_dim).astype(jnp.bfloat16)
    grad_pooled = loss_grad(pooled_low, labels)
    grad_scaled = grad_pooled.reshape(row_total, SEG, model_dim) / counts[:, :, None]
    grad_final = jnp.einsum(
        "rst,rsd->rtd", member, grad_scaled, precision=lax.Precision.HIGHEST
    ).reshape(token_count, model_dim)

    grad_gain_ffn = jnp.sum(grad_final * normed_ffn, axis=0)
    grad_shift_ffn = jnp.sum(grad_final, axis=0)
    grad_h2 = norm_back(grad_final * gain_ffn, normed_ffn, inv_ffn)
    grad_branch = grad_h2.astype(jnp.bfloat16)
    sent_c = swap(weight_grad("tall", 1, place, activ, grad_branch), "twin", 1)
    mine_c = weight_grad("tall", 0, place, activ, grad_branch)
    grad_b_outer = jnp.sum(grad_branch, axis=0, dtype=jnp.float32)
    mine_c, grad_branch = hold((mine_c, grad_branch))
    grad_inner = (back_dot(grad_branch, tall) * slope).astype(jnp.bfloat16)
    sent_c, grad_inner = hold((sent_c, grad_inner))
    other_c = swap(add_low(mine_c[:, 1], sent_c[:, 1]), "dp", 1)
    sent_b = swap(weight_grad("wide", 1, place, mid_low, grad_inner), "twin", 1)
    mine_b = weight_grad("wide", 0, place, mid_low, grad_inner)
    mine_b, grad_inner = hold((mine_b, grad_inner))
    grad_b_inner = jnp.sum(grad_inner, axis=0, dtype=jnp.float32)
    grad_mid = grad_h2 + back_dot(grad_inner, wide)
    sent_b, grad_mid = hold((sent_b, grad_mid))
    other_b = swap(add_low(mine_b[1], sent_b[1]), "dp", 2)
    grad_gain_attn = jnp.sum(grad_mid * normed_attn, axis=0)
    grad_shift_attn = jnp.sum(grad_mid, axis=0)
    grad_h1 = norm_back(grad_mid * gain_attn, normed_attn, inv_attn)
    grad_attn = grad_h1.astype(jnp.bfloat16)
    grad_b_out = jnp.sum(grad_attn, axis=0, dtype=jnp.float32)
    grad_ctx = back_dot(grad_attn, full_w_out).astype(jnp.bfloat16)
    other_c, grad_ctx = hold((other_c, grad_ctx))
    last_c = swap(add_low(mine_c[1, 0], sent_c[1, 0], other_c[1]), "dp", 2)
    grads = attend_back(seg_all, qkv, grad_ctx, log_total, grad_attn)
    last_c, other_b, grads = hold((last_c, other_b, grads))
    done_c = add_low(mine_c[0, 0], sent_c[0, 0], other_c[0], last_c)
    last_b = swap(add_low(mine_b[0, 1], sent_b[0, 1], other_b[1]), "dp", 1)
    parts_c = [swap(done_c[s], "fsdp", s) for s in (1, 2, 3)]
    sent_a = swap(weight_grad("square", 1, place, tok_ctx, grads), "twin", 1)
    mine_a = weight_grad("square", 0, place, tok_ctx, grads)
    last_b, parts_c, sent_a, mine_a, grads = hold((last_b, parts_c, sent_a, mine_a, grads))
    done_b = add_low(mine_b[0, 0], sent_b[0, 0], other_b[0], last_b)
    other_y = swap(add_low(mine_a[1, :, :2], sent_a[1, :, :2]), "dp", 2)
    other_x = swap(add_low(mine_a[:, 1, 2:], sent_a[:, 1, 2:]), "dp", 1)
    parts_b = [swap(done_b[s], "fsdp", s) for s in (1, 2, 3)]
    grad_b_query = jnp.sum(grads[0], axis=0, dtype=jnp.float32)
    grad_b_value = jnp.sum(grads[2], axis=0, dtype=jnp.float32)
    grad_tokens = project_back(grads, square, grad_h1)
    other_y, other_x, parts_b, grad_tokens = hold((other_y, other_x, parts_b, grad_tokens))
    grad_tokens = grad_tokens.reshape(row_total, seq_len, model_dim)
    last_y = swap(add_low(mine_a[0, 1, :2], sent_a[0, 1, :2], other_y[1]), "dp", 1)
    last_x = swap(add_low(mine_a[1, 0, 2:], sent_a[1, 0, 2:], other_x[1]), "dp", 2)
    back_cb = gather_back(
        jnp.stack([add_low(done_c[0], *parts_c), add_low(done_b[0], *parts_b)])
    )
    done_y = add_low(mine_a[0, 0, :2], sent_a[0, 0, :2], other_y[0], last_y)
    done_x = add_low(mine_a[0, 0, 2:], sent_a[0, 0, 2:], other_x[0], last_x)
    back_a = gather_back(
        add_low(
            done_y[0],
            swap(done_y[1], "fsdp", 1),
            swap(done_x[0], "fsdp", 2),
            swap(done_x[1], "fsdp", 3),
        )
    )

    vec = jnp.stack(
        [
            grad_b_query,
            grad_b_value,
            grad_b_out,
            grad_gain_attn,
            grad_shift_attn,
            grad_b_outer,
            grad_gain_ffn,
            grad_shift_ffn,
        ]
    )
    vec = jnp.concatenate([vec, grad_b_inner.reshape(4, model_dim)]).astype(jnp.bfloat16)
    for axis_name, bit in (("twin", 1), ("dp", 1), ("dp", 2)):
        vec = add_low(vec, swap(vec, axis_name, bit))
    vec = vec.astype(jnp.float32) + sum(
        swap(vec, "fsdp", s).astype(jnp.float32) for s in (1, 2, 3)
    )
    vec_small = lax.dynamic_slice(vec, (0, depth * shard), (8, shard))
    out_b_inner = lax.dynamic_index_in_dim(vec[8:], depth, 0, keepdims=False)

    outs = scatter_out(place, back_a, back_cb)
    return (
        output,
        grad_tokens,
        outs[0],
        vec_small[0],
        outs[1],
        outs[2],
        vec_small[1],
        outs[3],
        vec_small[2],
        vec_small[3],
        vec_small[4],
        outs[4],
        out_b_inner,
        outs[5],
        vec_small[5],
        vec_small[6],
        vec_small[7],
    )


def masked_scores(query, keys, seg_row):
    scores = jnp.einsum("qhd,khd->hqk", query, keys, preferred_element_type=jnp.float32) * HD ** (
        -0.5
    )
    same = seg_row[:, None] == seg_row[None, :]
    return jnp.where(same[None], scores, -1e30)


def attend_row(item):
    query, keys, values, seg_row = item
    scores = masked_scores(query, keys, seg_row)
    row_max = jnp.max(scores, axis=2, keepdims=True)
    exp_scores = jnp.exp(scores - row_max)
    row_sum = jnp.sum(exp_scores, axis=2, keepdims=True)
    attn_prob = (exp_scores / row_sum).astype(jnp.bfloat16)
    context = jnp.einsum("hqk,khd->qhd", attn_prob, values, preferred_element_type=jnp.float32)
    return (context.astype(jnp.bfloat16), row_max[:, :, 0] + jnp.log(row_sum[:, :, 0]))


def attend_row_back(item):
    query, keys, values, seg_row, log_total, grad_ctx = item
    attn_prob = jnp.exp(masked_scores(query, keys, seg_row) - log_total[:, :, None])
    grad_values = jnp.einsum(
        "hqk,qhd->khd", attn_prob.astype(jnp.bfloat16), grad_ctx, preferred_element_type=jnp.float32
    )
    grad_prob = jnp.einsum("qhd,khd->hqk", grad_ctx, values, preferred_element_type=jnp.float32)
    grad_scores = attn_prob * (grad_prob - jnp.sum(attn_prob * grad_prob, axis=2, keepdims=True))
    grad_scores = grad_scores.astype(jnp.bfloat16)
    grad_query = jnp.einsum(
        "hqk,khd->qhd", grad_scores, keys, preferred_element_type=jnp.float32
    ) * HD ** (-0.5)
    grad_keys = jnp.einsum(
        "hqk,qhd->khd", grad_scores, query, preferred_element_type=jnp.float32
    ) * HD ** (-0.5)
    return (
        grad_query.astype(jnp.bfloat16),
        grad_keys.astype(jnp.bfloat16),
        grad_values.astype(jnp.bfloat16),
    )


def forward_block(block_tok, seg_block, weights):
    (
        w_query,
        b_query,
        w_key,
        w_value,
        b_value,
        w_out,
        b_out,
        gain_attn,
        shift_attn,
        w_inner,
        b_inner,
        w_outer,
        b_outer,
        gain_ffn,
        shift_ffn,
    ) = weights
    row_count, seq_len, model_dim = block_tok.shape
    tok_flat = block_tok.reshape(row_count * seq_len, model_dim)
    head_shape = (row_count, seq_len, H, HD)
    query = (plain_dot(tok_flat, w_query) + b_query).astype(jnp.bfloat16).reshape(head_shape)
    keys = plain_dot(tok_flat, w_key).astype(jnp.bfloat16).reshape(head_shape)
    values = (plain_dot(tok_flat, w_value) + b_value).astype(jnp.bfloat16).reshape(head_shape)
    context, log_total = lax.map(attend_row, (query, keys, values, seg_block))
    context = context.reshape(row_count * seq_len, model_dim)
    normed_attn, inv_attn = normalize(
        tok_flat.astype(jnp.float32) + plain_dot(context, w_out) + b_out
    )
    mid_state = normed_attn * gain_attn + shift_attn
    mid_low = mid_state.astype(jnp.bfloat16)
    inner = plain_dot(mid_low, w_inner) + b_inner
    cdf_value, slope = gelu_parts(inner)
    activ = (inner * cdf_value).astype(jnp.bfloat16)
    normed_ffn, inv_ffn = normalize(mid_state + plain_dot(activ, w_outer) + b_outer)
    final = normed_ffn * gain_ffn + shift_ffn
    saved = (
        query,
        keys,
        values,
        log_total,
        context,
        normed_attn,
        inv_attn,
        mid_low,
        inner,
        activ,
        normed_ffn,
        inv_ffn,
    )
    return (final, saved)


def backward_block(grad_final, block_tok, seg_block, weights, saved):
    (
        w_query,
        b_query,
        w_key,
        w_value,
        b_value,
        w_out,
        b_out,
        gain_attn,
        shift_attn,
        w_inner,
        b_inner,
        w_outer,
        b_outer,
        gain_ffn,
        shift_ffn,
    ) = weights
    (
        query,
        keys,
        values,
        log_total,
        context,
        normed_attn,
        inv_attn,
        mid_low,
        inner,
        activ,
        normed_ffn,
        inv_ffn,
    ) = saved
    row_count, seq_len, model_dim = block_tok.shape
    tok_flat = block_tok.reshape(row_count * seq_len, model_dim)
    grad_gain_ffn = jnp.sum(grad_final * normed_ffn, axis=0)
    grad_shift_ffn = jnp.sum(grad_final, axis=0)
    grad_h2 = norm_back(grad_final * gain_ffn, normed_ffn, inv_ffn)
    grad_branch = grad_h2.astype(jnp.bfloat16)
    grad_w_outer = cross_dot(activ, grad_branch)
    grad_b_outer = jnp.sum(grad_branch, axis=0, dtype=jnp.float32)
    cdf_value, slope = gelu_parts(inner)
    grad_inner = (back_dot(grad_branch, w_outer) * slope).astype(jnp.bfloat16)
    grad_w_inner = cross_dot(mid_low, grad_inner)
    grad_b_inner = jnp.sum(grad_inner, axis=0, dtype=jnp.float32)
    grad_mid = grad_h2 + back_dot(grad_inner, w_inner)
    grad_gain_attn = jnp.sum(grad_mid * normed_attn, axis=0)
    grad_shift_attn = jnp.sum(grad_mid, axis=0)
    grad_h1 = norm_back(grad_mid * gain_attn, normed_attn, inv_attn)
    grad_attn = grad_h1.astype(jnp.bfloat16)
    grad_w_out = cross_dot(context, grad_attn)
    grad_b_out = jnp.sum(grad_attn, axis=0, dtype=jnp.float32)
    grad_ctx = back_dot(grad_attn, w_out).astype(jnp.bfloat16).reshape(row_count, seq_len, H, HD)
    grad_query, grad_keys, grad_values = lax.map(
        attend_row_back, (query, keys, values, seg_block, log_total, grad_ctx)
    )
    flat_shape = (row_count * seq_len, model_dim)
    grad_query = grad_query.reshape(flat_shape)
    grad_keys = grad_keys.reshape(flat_shape)
    grad_values = grad_values.reshape(flat_shape)
    grad_w_query = cross_dot(tok_flat, grad_query)
    grad_b_query = jnp.sum(grad_query, axis=0, dtype=jnp.float32)
    grad_w_key = cross_dot(tok_flat, grad_keys)
    grad_w_value = cross_dot(tok_flat, grad_values)
    grad_b_value = jnp.sum(grad_values, axis=0, dtype=jnp.float32)
    grad_tok = (
        grad_h1
        + back_dot(grad_query, w_query)
        + back_dot(grad_keys, w_key)
        + back_dot(grad_values, w_value)
    )
    grads = (
        grad_w_query,
        grad_b_query,
        grad_w_key,
        grad_w_value,
        grad_b_value,
        grad_w_out,
        grad_b_out,
        grad_gain_attn,
        grad_shift_attn,
        grad_w_inner,
        grad_b_inner,
        grad_w_outer,
        grad_b_outer,
        grad_gain_ffn,
        grad_shift_ffn,
    )
    return (grad_tok.astype(jnp.bfloat16).reshape(row_count, seq_len, model_dim), grads)


def reduce_grads(grads):
    (
        grad_w_query,
        grad_b_query,
        grad_w_key,
        grad_w_value,
        grad_b_value,
        grad_w_out,
        grad_b_out,
        grad_gain_attn,
        grad_shift_attn,
        grad_w_inner,
        grad_b_inner,
        grad_w_outer,
        grad_b_outer,
        grad_gain_ffn,
        grad_shift_ffn,
    ) = grads
    (
        shard_w_query,
        shard_b_query,
        shard_w_key,
        shard_w_value,
        shard_b_value,
        shard_w_out,
        shard_b_out,
        shard_gain_attn,
        shard_shift_attn,
        shard_w_inner,
        shard_b_inner,
        shard_w_outer,
        shard_b_outer,
        shard_gain_ffn,
        shard_shift_ffn,
    ) = (
        lax.psum_scatter(
            grad_w_query.astype(jnp.bfloat16), "fsdp", scatter_dimension=0, tiled=True
        ).astype(jnp.float32),
        lax.psum_scatter(
            grad_b_query.astype(jnp.bfloat16), "fsdp", scatter_dimension=0, tiled=True
        ).astype(jnp.float32),
        lax.psum_scatter(
            grad_w_key.astype(jnp.bfloat16), "fsdp", scatter_dimension=0, tiled=True
        ).astype(jnp.float32),
        lax.psum_scatter(
            grad_w_value.astype(jnp.bfloat16), "fsdp", scatter_dimension=0, tiled=True
        ).astype(jnp.float32),
        lax.psum_scatter(
            grad_b_value.astype(jnp.bfloat16), "fsdp", scatter_dimension=0, tiled=True
        ).astype(jnp.float32),
        lax.psum_scatter(
            grad_w_out.astype(jnp.bfloat16), "fsdp", scatter_dimension=0, tiled=True
        ).astype(jnp.float32),
        lax.psum_scatter(
            grad_b_out.astype(jnp.bfloat16), "fsdp", scatter_dimension=0, tiled=True
        ).astype(jnp.float32),
        lax.psum_scatter(
            grad_gain_attn.astype(jnp.bfloat16), "fsdp", scatter_dimension=0, tiled=True
        ).astype(jnp.float32),
        lax.psum_scatter(
            grad_shift_attn.astype(jnp.bfloat16), "fsdp", scatter_dimension=0, tiled=True
        ).astype(jnp.float32),
        lax.psum_scatter(
            grad_w_inner.astype(jnp.bfloat16), "fsdp", scatter_dimension=0, tiled=True
        ).astype(jnp.float32),
        lax.psum_scatter(
            grad_b_inner.astype(jnp.bfloat16), "fsdp", scatter_dimension=0, tiled=True
        ).astype(jnp.float32),
        lax.psum_scatter(
            grad_w_outer.astype(jnp.bfloat16), "fsdp", scatter_dimension=0, tiled=True
        ).astype(jnp.float32),
        lax.psum_scatter(
            grad_b_outer.astype(jnp.bfloat16), "fsdp", scatter_dimension=0, tiled=True
        ).astype(jnp.float32),
        lax.psum_scatter(
            grad_gain_ffn.astype(jnp.bfloat16), "fsdp", scatter_dimension=0, tiled=True
        ).astype(jnp.float32),
        lax.psum_scatter(
            grad_shift_ffn.astype(jnp.bfloat16), "fsdp", scatter_dimension=0, tiled=True
        ).astype(jnp.float32),
    )
    return (
        lax.psum(shard_w_query.astype(jnp.bfloat16), ("twin", "dp")).astype(jnp.float32),
        lax.psum(shard_b_query.astype(jnp.bfloat16), ("twin", "dp")).astype(jnp.float32),
        lax.psum(shard_w_key.astype(jnp.bfloat16), ("twin", "dp")).astype(jnp.float32),
        lax.psum(shard_w_value.astype(jnp.bfloat16), ("twin", "dp")).astype(jnp.float32),
        lax.psum(shard_b_value.astype(jnp.bfloat16), ("twin", "dp")).astype(jnp.float32),
        lax.psum(shard_w_out.astype(jnp.bfloat16), ("twin", "dp")).astype(jnp.float32),
        lax.psum(shard_b_out.astype(jnp.bfloat16), ("twin", "dp")).astype(jnp.float32),
        lax.psum(shard_gain_attn.astype(jnp.bfloat16), ("twin", "dp")).astype(jnp.float32),
        lax.psum(shard_shift_attn.astype(jnp.bfloat16), ("twin", "dp")).astype(jnp.float32),
        lax.psum(shard_w_inner.astype(jnp.bfloat16), ("twin", "dp")).astype(jnp.float32),
        lax.psum(shard_b_inner.astype(jnp.bfloat16), ("twin", "dp")).astype(jnp.float32),
        lax.psum(shard_w_outer.astype(jnp.bfloat16), ("twin", "dp")).astype(jnp.float32),
        lax.psum(shard_b_outer.astype(jnp.bfloat16), ("twin", "dp")).astype(jnp.float32),
        lax.psum(shard_gain_ffn.astype(jnp.bfloat16), ("twin", "dp")).astype(jnp.float32),
        lax.psum(shard_shift_ffn.astype(jnp.bfloat16), ("twin", "dp")).astype(jnp.float32),
    )


def general_device(
    tokens,
    w_query,
    b_query,
    w_key,
    w_value,
    b_value,
    w_out,
    b_out,
    gain_attn,
    shift_attn,
    w_inner,
    b_inner,
    w_outer,
    b_outer,
    gain_ffn,
    shift_ffn,
    lengths,
    labels,
):
    row_total, seq_len, model_dim = tokens.shape
    block_rows = row_total // MB
    seg_all = segment_ids(lengths, seq_len)
    member = (seg_all[:, None, :] == jnp.arange(SEG, dtype=jnp.int32)[None, :, None]).astype(
        jnp.float32
    )
    counts = lengths[:, :SEG].astype(jnp.float32)
    finals = []
    saved_list = []
    for block_idx in range(MB):
        row_span = slice(block_idx * block_rows, (block_idx + 1) * block_rows)
        weights = (
            lax.all_gather(w_query, "fsdp", axis=0, tiled=True),
            lax.all_gather(b_query, "fsdp", axis=0, tiled=True),
            lax.all_gather(w_key, "fsdp", axis=0, tiled=True),
            lax.all_gather(w_value, "fsdp", axis=0, tiled=True),
            lax.all_gather(b_value, "fsdp", axis=0, tiled=True),
            lax.all_gather(w_out, "fsdp", axis=0, tiled=True),
            lax.all_gather(b_out, "fsdp", axis=0, tiled=True),
            lax.all_gather(gain_attn, "fsdp", axis=0, tiled=True),
            lax.all_gather(shift_attn, "fsdp", axis=0, tiled=True),
            lax.all_gather(w_inner, "fsdp", axis=0, tiled=True),
            lax.all_gather(b_inner, "fsdp", axis=0, tiled=True),
            lax.all_gather(w_outer, "fsdp", axis=0, tiled=True),
            lax.all_gather(b_outer, "fsdp", axis=0, tiled=True),
            lax.all_gather(gain_ffn, "fsdp", axis=0, tiled=True),
            lax.all_gather(shift_ffn, "fsdp", axis=0, tiled=True),
        )
        final, saved = forward_block(tokens[row_span], seg_all[row_span], weights)
        finals.append(final.reshape(block_rows, seq_len, model_dim))
        saved_list.append(saved)
    final_all = jnp.concatenate(finals, axis=0)
    pooled_f = (
        jnp.einsum("rst,rtd->rsd", member, final_all, precision=lax.Precision.HIGHEST)
        / counts[:, :, None]
    )
    pooled_low = pooled_f.reshape(row_total * SEG, model_dim).astype(jnp.bfloat16)
    gathered = lax.all_gather(pooled_low, ("twin", "dp", "fsdp"), axis=0, tiled=True)
    own_count = pooled_low.shape[0]
    half_count = labels.shape[0]
    twin_side = lax.axis_index("twin")
    device = lax.axis_index(("twin", "dp", "fsdp"))
    first_seg = device * own_count
    other_start = (1 - twin_side) * half_count
    other_side = lax.dynamic_slice_in_dim(gathered, other_start, half_count, 0)
    own_f = pooled_low.astype(jnp.float32)
    other_f = other_side.astype(jnp.float32)
    inv_own = lax.rsqrt(jnp.sum(own_f * own_f, axis=1) + pool_eps)
    inv_other = lax.rsqrt(jnp.sum(other_f * other_f, axis=1) + pool_eps)
    col_index = jnp.arange(half_count, dtype=jnp.int32)
    similar = sim_scale * back_dot(pooled_low, other_side) * inv_own[:, None] * inv_other[None, :]
    own_labels = lax.dynamic_slice_in_dim(
        labels, jnp.minimum(first_seg, half_count - own_count), own_count, 0
    )
    own_index = first_seg - half_count + jnp.arange(own_count, dtype=jnp.int32)
    target = jnp.where(
        twin_side == 0,
        col_index[None, :] == own_labels[:, None],
        labels[None, :] == own_index[:, None],
    ).astype(jnp.float32)
    row_max = jnp.max(similar, axis=1, keepdims=True)
    log_total = row_max[:, 0] + jnp.log(jnp.sum(jnp.exp(similar - row_max), axis=1))
    grad_sim = jnp.exp(similar - log_total[:, None]) - target
    weighted = grad_sim * similar
    grad_raw = sim_scale * grad_sim * inv_own[:, None] * inv_other[None, :]
    grad_own = (
        jnp.dot(grad_raw, other_f, precision=lax.Precision.HIGHEST)
        - (jnp.sum(weighted, axis=1) * inv_own * inv_own)[:, None] * own_f
    )
    grad_other = (
        lax.dot_general(grad_raw, own_f, (((0,), (0,)), ((), ())), precision=lax.Precision.HIGHEST)
        - (jnp.sum(weighted, axis=0) * inv_other * inv_other)[:, None] * other_f
    )
    term = jnp.zeros((2 * half_count, model_dim), jnp.float32)
    term = lax.dynamic_update_slice_in_dim(term, grad_other, other_start, 0)
    term = lax.dynamic_update_slice_in_dim(term, grad_own, first_seg, 0)
    grad_pooled = lax.psum_scatter(term, ("twin", "dp", "fsdp"), scatter_dimension=0, tiled=True)
    grad_scaled = grad_pooled.reshape(row_total, SEG, model_dim) / counts[:, :, None]
    grad_toks = []
    grad_total = None
    for block_idx in range(MB):
        row_span = slice(block_idx * block_rows, (block_idx + 1) * block_rows)
        weights = (
            lax.all_gather(w_query, "fsdp", axis=0, tiled=True),
            lax.all_gather(b_query, "fsdp", axis=0, tiled=True),
            lax.all_gather(w_key, "fsdp", axis=0, tiled=True),
            lax.all_gather(w_value, "fsdp", axis=0, tiled=True),
            lax.all_gather(b_value, "fsdp", axis=0, tiled=True),
            lax.all_gather(w_out, "fsdp", axis=0, tiled=True),
            lax.all_gather(b_out, "fsdp", axis=0, tiled=True),
            lax.all_gather(gain_attn, "fsdp", axis=0, tiled=True),
            lax.all_gather(shift_attn, "fsdp", axis=0, tiled=True),
            lax.all_gather(w_inner, "fsdp", axis=0, tiled=True),
            lax.all_gather(b_inner, "fsdp", axis=0, tiled=True),
            lax.all_gather(w_outer, "fsdp", axis=0, tiled=True),
            lax.all_gather(b_outer, "fsdp", axis=0, tiled=True),
            lax.all_gather(gain_ffn, "fsdp", axis=0, tiled=True),
            lax.all_gather(shift_ffn, "fsdp", axis=0, tiled=True),
        )
        grad_final = jnp.einsum(
            "rst,rsd->rtd", member[row_span], grad_scaled[row_span], precision=lax.Precision.HIGHEST
        ).reshape(block_rows * seq_len, model_dim)
        grad_tok, grads = backward_block(
            grad_final, tokens[row_span], seg_all[row_span], weights, saved_list[block_idx]
        )
        grad_toks.append(grad_tok)
        grads = reduce_grads(grads)
        grad_total = grads if grad_total is None else jax.tree.map(jnp.add, grad_total, grads)
    output = final_all.astype(jnp.bfloat16)
    grad_tokens = jnp.concatenate(grad_toks, axis=0)
    return (output, grad_tokens) + tuple(grad_total)


def solution(mesh):
    placed = (
        P(("twin", "dp", "fsdp"), None, None),
        P("fsdp", None),
        P("fsdp"),
        P("fsdp", None),
        P("fsdp", None),
        P("fsdp"),
        P("fsdp", None),
        P("fsdp"),
        P("fsdp"),
        P("fsdp"),
        P("fsdp", None),
        P("fsdp"),
        P("fsdp", None),
        P("fsdp"),
        P("fsdp"),
        P("fsdp"),
        P(("twin", "dp", "fsdp"), None),
        P(),
    )
    sizes = (mesh.shape["twin"], mesh.shape["dp"], mesh.shape["fsdp"])
    return jax.shard_map(
        per_device if sizes == (2, 4, 4) else general_device,
        mesh=mesh,
        in_specs=placed,
        out_specs=(
            P(("twin", "dp", "fsdp"), None, None),
            P(("twin", "dp", "fsdp"), None, None),
            P("fsdp", None),
            P("fsdp"),
            P("fsdp", None),
            P("fsdp", None),
            P("fsdp"),
            P("fsdp", None),
            P("fsdp"),
            P("fsdp"),
            P("fsdp"),
            P("fsdp", None),
            P("fsdp"),
            P("fsdp", None),
            P("fsdp"),
            P("fsdp"),
            P("fsdp"),
        ),
        check_vma=False,
    )
```
